512 devices in a mesh: wa: 128 (over z, x, y_hi), gx: 4 (over y_lo, core).
Axes of the slice: x: 4, y: 4 (y_hi: 2, y_lo: 2; y = y_hi * 2 + y_lo), z: 16, core: 2. Of those that a mesh axis runs over, the one named last changes fastest.
Arguments:
- field_a: float32 [2, 4, 768, 3840], P(None, 'gx', 'wa'), may hold values from -6 to 6
- field_b: float32 [2, 4, 768, 3840], P(None, 'gx', 'wa'), may hold values from -6 to 6
- keep_mask: int32 [3840], replicated, may hold values 0 or 1
- block_inv: float32 [6, 128, 128], replicated
- lower_mult: float32 [5, 128, 128], replicated, may hold values from -0.15 to 0.15
Outputs:
- new_a: float32 [2, 4, 768, 3840], P(None, 'gx', 'wa')
- new_b: float32 [2, 4, 768, 3840], P(None, 'gx', 'wa')
The draws below stay inside these ranges and needn't reach their ends.
All inputs are finite; a program needn't handle non-finite values.
Results may differ from the reference program's by a relative error of at most 0.0001.
Values sent between devices are 32-bit elements; how exact they have to be, the bound alone decides.
No kernel may reach another device: no remote copies, remote signals or barrier semaphores. Data moves between devices by JAX's collectives and lax.ppermute only.
A program may use at most 64 MiB of HBM per device.

```python
import math
import jax
import jax.numpy as jnp
from jax import lax

NKZ = 3840
NY = 768
BLK = 128
NZ = 5760
NB = 6
KXT = 4


def draw_block_inv(key, part):
    own_key = jax.random.fold_in(key, 11)
    diag_key, rest_key = jax.random.split(own_key)
    diagonal = jnp.exp(jax.random.uniform(diag_key, (NB, BLK), jnp.float32, -0.6931, 0.6931))
    offdiag = jax.random.normal(rest_key, (NB, BLK, BLK), jnp.float32) * 0.03
    return offdiag + diagonal[:, :, None] * jnp.eye(BLK, dtype=jnp.float32)[None]


def set_ends(values, stream_key, smallest, top_value):
    longest = values.shape.index(max(values.shape))
    spots = []
    for shift in (0, 1):
        where = [jax.random.randint(jax.random.fold_in(stream_key, axis), (), 0, length) for axis, length in enumerate(values.shape)]
        where[longest] = (where[longest] + shift) % values.shape[longest]
        spots.append(tuple(where))
    return values.at[spots[0]].set(smallest).at[spots[1]].set(top_value)


def level_of(key, dims, shards, smallest, top_value):
    factor_of, own = 1.0, jax.random.fold_in(key, 6)
    for dim, shards_of in shards:
        draws = jnp.exp(jax.random.uniform(jax.random.fold_in(own, dim), (shards_of,), jnp.float32, smallest / len(shards), top_value / len(shards)))
        factor_of = factor_of * jnp.repeat(draws, dims[dim] // shards_of).reshape([-1 if axis == dim else 1 for axis in range(len(dims))])
    return factor_of


def centred(key, extent, scale, limit, cuts=(), kind=jnp.bfloat16):
    loudness = level_of(key, extent, cuts, -0.22, 0.18) if cuts else 1.0
    array = jax.random.normal(key, extent, jnp.float32) * scale * loudness
    return jnp.minimum(jnp.maximum(array, -limit), limit).astype(kind)


def setup_inputs(seed: int = 0) -> dict:
    keys = jax.random.split(jax.random.key(seed), 6)
    return {
        "field_a": centred(keys[0], (2, KXT, NY, NKZ), 1.0, 6.0, ((1, 4), (2, 128)), jnp.float32),
        "field_b": centred(keys[1], (2, KXT, NY, NKZ), 1.0, 6.0, ((1, 4), (2, 128)), jnp.float32),
        "keep_mask": set_ends((jax.random.randint(keys[2], (NKZ,), 0, 8) < 7).astype(jnp.int32), jax.random.fold_in(keys[2], 1), 0, 1),
        "block_inv": draw_block_inv(jax.random.fold_in(keys[5], 71), 0),
        "lower_mult": centred(keys[4], (NB - 1, BLK, BLK), 0.025, 0.15, (), jnp.float32),
    }


NL_COEFF = 0.25

def to_grid(field):
    half = NKZ // 2
    spectra = lax.complex(field[0], field[1])
    padding = jnp.zeros(spectra.shape[:-1] + (NZ - NKZ,), spectra.dtype)
    padded = jnp.concatenate([spectra[..., :half], padding, spectra[..., half:]], axis=-1)
    values = jnp.fft.ifft(padded, axis=-1) * (NZ / math.sqrt(NKZ))
    return (jnp.real(values), jnp.imag(values))

def to_modes(real_part, imag_part):
    half = NKZ // 2
    values = jnp.fft.fft(lax.complex(real_part, imag_part), axis=-1) / math.sqrt(NZ)
    kept = jnp.concatenate([values[..., :half], values[..., NZ - half:]], axis=-1)
    return (jnp.real(kept), jnp.imag(kept))

def complex_product(left_re, left_im, right_re, right_im):
    return (left_re * right_re - left_im * right_im, left_re * right_im + left_im * right_re)

def front(slab_a, slab_b, keep):
    a_re, a_im = to_grid(slab_a)
    b_re, b_im = to_grid(slab_b)
    p_re = jnp.zeros_like(a_re)
    p_im = jnp.zeros_like(a_re)
    q_re = jnp.zeros_like(a_re)
    q_im = jnp.zeros_like(a_re)
    for offset in range(KXT):
        ra_re = jnp.roll(a_re, offset, axis=0)
        ra_im = jnp.roll(a_im, offset, axis=0)
        rb_re = jnp.roll(b_re, offset, axis=0)
        rb_im = jnp.roll(b_im, offset, axis=0)
        ab_re, ab_im = complex_product(a_re[offset], a_im[offset], rb_re, rb_im)
        aa_re, aa_im = complex_product(a_re[offset], a_im[offset], ra_re, ra_im)
        bb_re, bb_im = complex_product(b_re[offset], b_im[offset], rb_re, rb_im)
        p_re = p_re + ab_re
        p_im = p_im + ab_im
        q_re = q_re + aa_re - bb_re
        q_im = q_im + aa_im - bb_im
    hp_re, hp_im = to_modes(p_re, p_im)
    hq_re, hq_im = to_modes(q_re, q_im)
    rhs_a = slab_a + NL_COEFF * jnp.stack([hp_re, hp_im]) * keep
    rhs_b = slab_b + NL_COEFF * jnp.stack([hq_re, hq_im]) * keep
    return (rhs_a, rhs_b)

def solve_rows(rhs, block_inv, lower_mult):
    shape = rhs.shape
    nblocks = block_inv.shape[0]
    width = block_inv.shape[1]
    vectors = jnp.swapaxes(rhs, 2, 3).reshape(-1, nblocks, width)
    blocks = jnp.moveaxis(vectors, 1, 0)

    def forward(previous, inputs):
        current, multiplier = inputs
        result = current - jnp.einsum('mc,rc->mr', previous, multiplier, precision=lax.Precision.HIGHEST)
        return (result, result)
    _, later = lax.scan(forward, blocks[0], (blocks[1:], lower_mult))
    reduced = jnp.concatenate([blocks[:1], later], axis=0)
    last = jnp.einsum('mc,rc->mr', reduced[-1], block_inv[-1], precision=lax.Precision.HIGHEST)

    def backward(following, inputs):
        current, inverse, multiplier = inputs
        result = jnp.einsum('mc,rc->mr', current, inverse, precision=lax.Precision.HIGHEST)
        result = result - jnp.einsum('mc,cr->mr', following, multiplier, precision=lax.Precision.HIGHEST)
        return (result, result)
    _, earlier = lax.scan(backward, last, (reduced[:-1], block_inv[:-1], lower_mult), reverse=True)
    solved = jnp.concatenate([earlier, last[None]], axis=0)
    solved = jnp.moveaxis(solved, 0, 1).reshape(shape[0], shape[1], shape[3], shape[2])
    return jnp.swapaxes(solved, 2, 3)

def reference(field_a, field_b, keep_mask, block_inv, lower_mult):
    keep = keep_mask.astype(field_a.dtype)
    rows = math.gcd(NY, 128)
    count = NY // rows

    def split(field):
        return jnp.moveaxis(field.reshape(2, KXT, count, rows, NKZ), 2, 0)

    def merge_back(blocks):
        return jnp.moveaxis(blocks, 0, 2).reshape(2, KXT, NY, NKZ)

    def one_block(pair):
        return front(pair[0], pair[1], keep)
    rhs_a, rhs_b = lax.map(one_block, (split(field_a), split(field_b)))
    new_a = solve_rows(merge_back(rhs_a), block_inv, lower_mult)
    new_b = solve_rows(merge_back(rhs_b), block_inv, lower_mult)
    return (new_a, new_b)
```

```python
import math

import jax
import jax.numpy as jnp
import ml_dtypes
import numpy as np
from jax import lax
from jax.experimental import pallas as pl
from jax.experimental.pallas import tpu as pltpu
from jax.sharding import PartitionSpec as P

NL_COEFF = 0.25
BF16 = ml_dtypes.bfloat16

LANES = 128
OUTER = 45
KEPT = 30
ROWS = 6
SLOT = 48
PARTS = 2 * ROWS * KEPT


def split_np(table):
    high = table.astype(np.float32).astype(BF16)
    low = (table - high.astype(np.float64)).astype(np.float32).astype(BF16)
    return high, low


def build_tables():
    modes = KEPT * LANES
    length = OUTER * LANES
    half = KEPT // 2
    kept = np.array([j if j < half else j + OUTER - KEPT for j in range(KEPT)])
    n1 = np.arange(OUTER)
    lane = np.arange(LANES)
    short = 2.0 * np.pi * ((n1[:, None] * kept[None, :]) % OUTER) / OUTER
    to_grid = np.zeros((2 * SLOT, 64))
    scale = 1.0 / math.sqrt(modes)
    to_grid[:OUTER, 0:KEPT] = np.cos(short) * scale
    to_grid[:OUTER, 34:64] = -np.sin(short) * scale
    to_grid[SLOT : SLOT + OUTER, 0:KEPT] = np.sin(short) * scale
    to_grid[SLOT : SLOT + OUTER, 34:64] = np.cos(short) * scale
    to_modes = np.zeros((64, 2 * SLOT))
    scale = NL_COEFF / math.sqrt(length)
    to_modes[0:KEPT, :OUTER] = np.cos(short).T * scale
    to_modes[0:KEPT, SLOT : SLOT + OUTER] = -np.sin(short).T * scale
    to_modes[34:64, :OUTER] = -np.sin(short).T * scale
    to_modes[34:64, SLOT : SLOT + OUTER] = -np.cos(short).T * scale
    twist = 2.0 * np.pi * (n1[:, None] * lane[None, :]) / length
    twist_re = np.zeros((SLOT, LANES), np.float32)
    twist_im = np.zeros((SLOT, LANES), np.float32)
    twist_re[:OUTER] = np.cos(twist)
    twist_im[:OUTER] = np.sin(twist)
    long = 2.0 * np.pi * ((lane[:, None] * lane[None, :]) % LANES) / LANES
    cos, sin = np.cos(long), np.sin(long)
    lanes = np.block([[cos, sin], [-sin, cos]])
    grid_h, grid_l = split_np(to_grid)
    modes_h, modes_l = split_np(to_modes)
    lanes_h, lanes_l = split_np(lanes)
    return dict(
        to_grid=np.concatenate([grid_h, grid_h, grid_l], axis=1),
        to_modes=np.concatenate([modes_h, modes_h, modes_l], axis=1),
        twist_re=twist_re,
        twist_im=twist_im,
        lanes_h=lanes_h,
        lanes_l=lanes_l,
    )


def dot(left, right):
    return jnp.dot(left, right, preferred_element_type=jnp.float32)


def split(value):
    high = value.astype(jnp.bfloat16)
    low = (value - high.astype(jnp.float32)).astype(jnp.bfloat16)
    return high, low


def load_modes(w_ref, field, row):
    base = field * PARTS + KEPT * row
    re = w_ref[pl.ds(base, 32), :]
    im = w_ref[pl.ds(base + PARTS // 2 - 2, 32), :]
    return jnp.concatenate([re, im], axis=0)


def lane_transform(high_ref, low_ref, lanes_h_ref, lanes_l_ref):
    table = lanes_h_ref[...]
    return (
        dot(high_ref[...], table) + dot(low_ref[...], table) + dot(high_ref[...], lanes_l_ref[...])
    )


def grid_kernel(w_ref, table_ref, twr_ref, twi_ref, lh_ref, ll_ref, out_ref, uh_ref, ul_ref):
    table = table_ref[...]
    twr, twi = twr_ref[...], twi_ref[...]
    for row in range(ROWS):
        modes = jnp.concatenate([load_modes(w_ref, 0, row), load_modes(w_ref, 1, row)], axis=1)
        high, low = split(modes)
        sums = dot(table, jnp.concatenate([high, low, high], axis=0))
        for field in range(2):
            lanes = slice(field * LANES, (field + 1) * LANES)
            re, im = sums[:SLOT, lanes], sums[SLOT:, lanes]
            twisted = jnp.concatenate([re * twr - im * twi, re * twi + im * twr], axis=1)
            high, low = split(twisted)
            rows = pl.ds((2 * row + field) * SLOT, SLOT)
            uh_ref[rows, :] = high
            ul_ref[rows, :] = low
    out_ref[...] = lane_transform(uh_ref, ul_ref, lh_ref, ll_ref)


def to_grid(own, tables):
    rows = 2 * ROWS * SLOT
    return pl.pallas_call(
        grid_kernel,
        out_shape=jax.ShapeDtypeStruct((rows, 2 * LANES), jnp.float32),
        scratch_shapes=[pltpu.VMEM((rows, 2 * LANES), jnp.bfloat16)] * 2,
        cost_estimate=pl.CostEstimate(
            flops=2 * rows * 256 * 256 * 3, bytes_accessed=1400000, transcendentals=0
        ),
        name="to_grid",
    )(
        own,
        tables["to_grid"],
        tables["twist_re"],
        tables["twist_im"],
        tables["lanes_h"],
        tables["lanes_l"],
    )


def pairs_of(x):
    return [(j ^ x, ((x - j) % 4) ^ x) for j in range(4)]


def complex_product(left, right):
    return (left[0] * right[0] - left[1] * right[1], left[0] * right[1] + left[1] * right[0])


def modes_kernel(
    x_ref, g0, g1, g2, g3, w_ref, mask_ref, table_ref, twr_ref, twi_ref, lh_ref, ll_ref,
    out_ref, uh_ref, ul_ref,
):
    grids = (g0, g1, g2, g3)
    x = x_ref[0]
    step_rows = 16

    def convolve(pairs):
        def step(index, carry):
            row = index // 3
            base = row * 2 * SLOT + (index - row * 3) * step_rows

            def load(grid, field):
                rows = pl.ds(pl.multiple_of(base + field * SLOT, step_rows), step_rows)
                return (grid[rows, pl.ds(0, LANES)], grid[rows, pl.ds(LANES, LANES)])

            a = [load(grid, 0) for grid in grids]
            b = [load(grid, 1) for grid in grids]
            p = q = None
            for left, right in pairs:
                ab = complex_product(a[left], b[right])
                aa = complex_product(a[left], a[right])
                bb = complex_product(b[left], b[right])
                if p is None:
                    p = ab
                    q = (aa[0] - bb[0], aa[1] - bb[1])
                else:
                    p = (p[0] + ab[0], p[1] + ab[1])
                    q = (q[0] + aa[0] - bb[0], q[1] + aa[1] - bb[1])
            for field, (re, im) in enumerate((p, q)):
                high, low = split(jnp.concatenate([re, -im], axis=1))
                rows = pl.ds(pl.multiple_of(base + field * SLOT, step_rows), step_rows)
                uh_ref[rows, :] = high
                ul_ref[rows, :] = low
            return carry

        lax.fori_loop(0, 3 * ROWS, step, 0)

    for value in range(4):

        @pl.when(x == value)
        def _(value=value):
            convolve(pairs_of(value))

    spectra = lane_transform(uh_ref, ul_ref, lh_ref, ll_ref)
    table = table_ref[...]
    twr, twi = twr_ref[...], twi_ref[...]
    mask = mask_ref[...]
    for row in range(ROWS):
        re_parts, im_parts = [], []
        for field in range(2):
            start = (2 * row + field) * SLOT
            re = spectra[start : start + SLOT, :LANES]
            im = spectra[start : start + SLOT, LANES:]
            re_parts.append(re * twr - im * twi)
            im_parts.append(re * twi + im * twr)
        twisted = jnp.concatenate(
            [jnp.concatenate(re_parts, axis=1), jnp.concatenate(im_parts, axis=1)], axis=0
        )
        high, low = split(twisted)
        hat = dot(table, jnp.concatenate([high, low, high], axis=0))
        columns = jnp.concatenate(
            [
                load_modes(w_ref, field, row)
                + hat[:, field * LANES : (field + 1) * LANES] * mask
                for field in range(2)
            ],
            axis=0,
        )
        out_ref[pl.ds(row, LANES, stride=ROWS), :] = columns.T


def to_rhs(x, grids, own, mask, tables):
    rows = 2 * ROWS * SLOT
    vmem = pl.BlockSpec(memory_space=pltpu.VMEM)
    return pl.pallas_call(
        modes_kernel,
        out_shape=jax.ShapeDtypeStruct((ROWS * LANES, LANES), jnp.float32),
        in_specs=[pl.BlockSpec(memory_space=pltpu.SMEM)] + [vmem] * 11,
        out_specs=vmem,
        scratch_shapes=[pltpu.VMEM((rows, 2 * LANES), jnp.bfloat16)] * 2,
        cost_estimate=pl.CostEstimate(
            flops=2 * rows * 256 * 256 * 3, bytes_accessed=3500000, transcendentals=0
        ),
        name="to_rhs",
    )(
        x,
        *grids,
        own,
        mask,
        tables["to_modes"],
        tables["twist_re"],
        tables["twist_im"],
        tables["lanes_h"],
        tables["lanes_l"],
    )


def matmul3(left, right, contract=((1,), (0,))):
    left_h, left_l = split(left)
    right_h, right_l = split(right)

    def one(u, v):
        return lax.dot_general(u, v, (contract, ((), ())), preferred_element_type=jnp.float32)

    return one(left_h, right_h) + one(left_h, right_l) + one(left_l, right_h)


def operator_kernel(inv_ref, mult_ref, high_ref, low_ref, g_ref, s_ref):
    nblocks, width, _ = inv_ref.shape
    eye = (
        lax.broadcasted_iota(jnp.int32, (width, width), 0)
        == lax.broadcasted_iota(jnp.int32, (width, width), 1)
    ).astype(jnp.float32)
    for j in range(nblocks):
        rows = pl.ds(j * width, width)
        if j:
            g_ref[rows, : j * width] = -matmul3(
                mult_ref[j - 1], g_ref[pl.ds((j - 1) * width, width), : j * width]
            )
        g_ref[rows, j * width : (j + 1) * width] = eye
    for j in reversed(range(nblocks)):
        rows = pl.ds(j * width, width)
        own = (j + 1) * width
        result = matmul3(inv_ref[j], g_ref[rows, :own])
        if j < nblocks - 1:
            result = jnp.concatenate(
                [result, jnp.zeros((width, (nblocks - 1 - j) * width), jnp.float32)], axis=1
            )
            result = result - matmul3(
                mult_ref[j], s_ref[pl.ds((j + 1) * width, width), :], ((0,), (0,))
            )
        s_ref[rows, :] = result
        high, low = split(result)
        high_ref[rows, :] = high
        low_ref[rows, :] = low


def solve_operator(block_inv, lower_mult):
    size = block_inv.shape[0] * block_inv.shape[1]
    return pl.pallas_call(
        operator_kernel,
        out_shape=[jax.ShapeDtypeStruct((size, size), jnp.bfloat16)] * 2,
        scratch_shapes=[pltpu.VMEM((size, size), jnp.float32)] * 2,
        cost_estimate=pl.CostEstimate(
            flops=2 * 55 * 3 * 128**3 * 4, bytes_accessed=3100000, transcendentals=0
        ),
        name="solve_operator",
    )(block_inv, lower_mult)


def solve_kernel(high_ref, low_ref, r_ref, out_ref):
    high, low = split(r_ref[...])
    both = dot(high_ref[...], jnp.concatenate([high, low], axis=1))
    out_ref[...] = both[:, :LANES] + both[:, LANES:] + dot(low_ref[...], high)


def solve(operator, rhs):
    return pl.pallas_call(
        solve_kernel,
        out_shape=jax.ShapeDtypeStruct(rhs.shape, jnp.float32),
        name="solve",
    )(*operator, rhs)


def spread_kernel(s_ref, a_ref, b_ref):
    for row in range(ROWS):
        columns = s_ref[pl.ds(row, LANES, stride=ROWS), :].T
        for field, ref in enumerate((a_ref, b_ref)):
            base = field * 64
            ref[pl.ds(row * KEPT, KEPT), :] = columns[base : base + KEPT]
            ref[pl.ds(PARTS // 2 + row * KEPT, KEPT), :] = columns[base + 34 : base + 64]


def spread(solved):
    return pl.pallas_call(
        spread_kernel,
        out_shape=[jax.ShapeDtypeStruct((PARTS, LANES), jnp.float32)] * 2,
        name="spread",
    )(solved)


def exchange(rows):
    count = rows.shape[0] // ROWS
    sent = rows.reshape(count, 1, ROWS * LANES)
    return lax.all_to_all(sent, "wa", 0, 0, tiled=True).reshape(rows.shape)


def permute(value, flip):
    return lax.ppermute(value, "gx", [(i, i ^ flip) for i in range(4)])


def body(field_a, field_b, keep_mask, block_inv, lower_mult):
    tables = {name: jnp.asarray(table) for name, table in build_tables().items()}
    own = jnp.concatenate([field_a.reshape(PARTS, LANES), field_b.reshape(PARTS, LANES)], axis=0)
    keep = keep_mask.astype(jnp.float32).reshape(KEPT, LANES)
    gap = jnp.zeros((2, LANES), jnp.float32)
    mask = jnp.concatenate([keep, gap, gap, keep], axis=0)
    x = lax.axis_index("gx").astype(jnp.int32).reshape(1)

    two = permute(own, 2)
    one = permute(own, 1)
    three = permute(two, 1)
    operator = solve_operator(block_inv, lower_mult)
    grids = [to_grid(part, tables) for part in (own, one, two, three)]
    rhs = to_rhs(x, grids, own, mask, tables)
    solved = solve(operator, exchange(rhs))
    new_a, new_b = spread(exchange(solved))
    return (new_a.reshape(field_a.shape), new_b.reshape(field_b.shape))


def solution(mesh):
    return jax.shard_map(
        body,
        mesh=mesh,
        in_specs=(P(None, "gx", "wa", None), P(None, "gx", "wa", None), P(), P(), P()),
        out_specs=(P(None, "gx", "wa", None), P(None, "gx", "wa", None)),
        check_vma=False,
    )
```

```python
import math

import jax
import jax.numpy as jnp
import ml_dtypes
import numpy as np
from jax import lax
from jax.experimental import pallas as pl
from jax.experimental.pallas import tpu as pltpu
from jax.sharding import Mesh
from jax.sharding import PartitionSpec as P

NL_COEFF = 0.25
BF16 = ml_dtypes.bfloat16

LANES = 128
OUTER = 45
KEPT = 30
ROWS = 6
HALF = ROWS // 2
SLOT = 48
PADDED = 64
PARTS = 2 * ROWS * KEPT


def split_np(table):
    high = table.astype(np.float32).astype(BF16)
    low = (table - high.astype(np.float64)).astype(np.float32).astype(BF16)
    return high, low


def build_tables():
    modes = KEPT * LANES
    length = OUTER * LANES
    half = KEPT // 2
    kept = np.array([j if j < half else j + OUTER - KEPT for j in range(KEPT)])
    n1 = np.arange(OUTER)
    lane = np.arange(LANES)
    short = 2.0 * np.pi * ((n1[:, None] * kept[None, :]) % OUTER) / OUTER
    to_grid = np.zeros((2 * SLOT, 64))
    scale = 1.0 / math.sqrt(modes)
    to_grid[:OUTER, 0:KEPT] = np.cos(short) * scale
    to_grid[:OUTER, 34:64] = -np.sin(short) * scale
    to_grid[SLOT : SLOT + OUTER, 0:KEPT] = np.sin(short) * scale
    to_grid[SLOT : SLOT + OUTER, 34:64] = np.cos(short) * scale
    to_modes = np.zeros((64, 2 * SLOT))
    scale = NL_COEFF / math.sqrt(length)
    to_modes[0:KEPT, :OUTER] = np.cos(short).T * scale
    to_modes[0:KEPT, SLOT : SLOT + OUTER] = -np.sin(short).T * scale
    to_modes[34:64, :OUTER] = -np.sin(short).T * scale
    to_modes[34:64, SLOT : SLOT + OUTER] = -np.cos(short).T * scale
    twist = 2.0 * np.pi * (n1[:, None] * lane[None, :]) / length
    twist_re = np.zeros((SLOT, LANES), np.float32)
    twist_im = np.zeros((SLOT, LANES), np.float32)
    twist_re[:OUTER] = np.cos(twist)
    twist_im[:OUTER] = np.sin(twist)
    long = 2.0 * np.pi * ((lane[:, None] * lane[None, :]) % LANES) / LANES
    cos, sin = np.cos(long), np.sin(long)
    lanes = np.block([[cos, sin], [-sin, cos]])
    grid_h, grid_l = split_np(to_grid)
    modes_h, modes_l = split_np(to_modes)
    lanes_h, lanes_l = split_np(lanes)
    return dict(
        to_grid=np.concatenate([grid_h, grid_h, grid_l], axis=1),
        to_modes=np.concatenate([modes_h, modes_h, modes_l], axis=1),
        twist_re=twist_re,
        twist_im=twist_im,
        lanes_h=lanes_h,
        lanes_l=lanes_l,
    )


def dot(left, right):
    return jnp.dot(left, right, preferred_element_type=jnp.float32)


def split(value):
    high = value.astype(jnp.bfloat16)
    low = (value - high.astype(jnp.float32)).astype(jnp.bfloat16)
    return high, low


def prepare_kernel(y_ref, a_ref, b_ref, send_ref, keep_ref):
    mine = y_ref[0]
    for half, out_ref in ((1 - mine, send_ref), (mine, keep_ref)):
        for field, ref in enumerate((a_ref, b_ref)):
            for i in range(HALF):
                base = half * (HALF * KEPT) + i * KEPT
                row = (field * HALF + i) * PADDED
                out_ref[pl.ds(row, 32), :] = ref[pl.ds(base, 32), :]
                out_ref[pl.ds(row + 32, 32), :] = ref[pl.ds(base + PARTS // 2 - 2, 32), :]


def prepare(y, field_a, field_b):
    vmem = pl.BlockSpec(memory_space=pltpu.VMEM)
    shape = jax.ShapeDtypeStruct((2 * HALF * PADDED, LANES), jnp.float32)
    return pl.pallas_call(
        prepare_kernel,
        out_shape=[shape, shape],
        in_specs=[pl.BlockSpec(memory_space=pltpu.SMEM), vmem, vmem],
        out_specs=[vmem, vmem],
        name="prepare",
    )(y, field_a, field_b)


def load_modes(w_ref, field, i):
    return w_ref[pl.ds((field * HALF + i) * PADDED, PADDED), :]


def lane_transform(high_ref, low_ref, lanes_h_ref, lanes_l_ref):
    table = lanes_h_ref[...]
    return (
        dot(high_ref[...], table) + dot(low_ref[...], table) + dot(high_ref[...], lanes_l_ref[...])
    )


def grid_kernel(w_ref, table_ref, twr_ref, twi_ref, lh_ref, ll_ref, out_ref, uh_ref, ul_ref):
    table = table_ref[...]
    twr, twi = twr_ref[...], twi_ref[...]
    for row in range(HALF):
        modes = jnp.concatenate([load_modes(w_ref, 0, row), load_modes(w_ref, 1, row)], axis=1)
        high, low = split(modes)
        sums = dot(table, jnp.concatenate([high, low, high], axis=0))
        for field in range(2):
            lanes = slice(field * LANES, (field + 1) * LANES)
            re, im = sums[:SLOT, lanes], sums[SLOT:, lanes]
            twisted = jnp.concatenate([re * twr - im * twi, re * twi + im * twr], axis=1)
            high, low = split(twisted)
            rows = pl.ds((2 * row + field) * SLOT, SLOT)
            uh_ref[rows, :] = high
            ul_ref[rows, :] = low
    out_ref[...] = lane_transform(uh_ref, ul_ref, lh_ref, ll_ref)


def to_grid(own, tables):
    rows = 2 * HALF * SLOT
    return pl.pallas_call(
        grid_kernel,
        out_shape=jax.ShapeDtypeStruct((rows, 2 * LANES), jnp.float32),
        scratch_shapes=[pltpu.VMEM((rows, 2 * LANES), jnp.bfloat16)] * 2,
        cost_estimate=pl.CostEstimate(
            flops=2 * rows * 256 * 256 * 3, bytes_accessed=900000, transcendentals=0
        ),
        name="to_grid",
    )(
        own,
        tables["to_grid"],
        tables["twist_re"],
        tables["twist_im"],
        tables["lanes_h"],
        tables["lanes_l"],
    )


def pairs_of(x, target):
    return [(j ^ x, ((target - j) % 4) ^ x) for j in range(4)]


def complex_product(left, right):
    return (left[0] * right[0] - left[1] * right[1], left[0] * right[1] + left[1] * right[0])


def modes_kernel(
    x_ref, g0, g1, g2, g3, w0_ref, w2_ref, mask_ref, table_ref, twr_ref, twi_ref, lh_ref, ll_ref,
    out_ref, uh_ref, ul_ref,
):
    grids = (g0, g1, g2, g3)
    x = x_ref[0]
    step_rows = 16

    def convolve(all_pairs):
        def step(index, carry):
            row = index // 3
            part = (index - row * 3) * step_rows
            base = row * 2 * SLOT + part

            def load(grid, field):
                rows = pl.ds(pl.multiple_of(base + field * SLOT, step_rows), step_rows)
                return (grid[rows, pl.ds(0, LANES)], grid[rows, pl.ds(LANES, LANES)])

            a = [load(grid, 0) for grid in grids]
            b = [load(grid, 1) for grid in grids]
            for target, pairs in enumerate(all_pairs):
                p = q = None
                for left, right in pairs:
                    ab = complex_product(a[left], b[right])
                    aa = complex_product(a[left], a[right])
                    bb = complex_product(b[left], b[right])
                    if p is None:
                        p = ab
                        q = (aa[0] - bb[0], aa[1] - bb[1])
                    else:
                        p = (p[0] + ab[0], p[1] + ab[1])
                        q = (q[0] + aa[0] - bb[0], q[1] + aa[1] - bb[1])
                for field, (re, im) in enumerate((p, q)):
                    high, low = split(jnp.concatenate([re, -im], axis=1))
                    start = base + (target * 2 * HALF + field) * SLOT
                    rows = pl.ds(pl.multiple_of(start, step_rows), step_rows)
                    uh_ref[rows, :] = high
                    ul_ref[rows, :] = low
            return carry

        lax.fori_loop(0, 3 * HALF, step, 0)

    for value in range(4):

        @pl.when(x == value)
        def _(value=value):
            convolve([pairs_of(value, 2 * target + value % 2) for target in range(2)])

    spectra = lane_transform(uh_ref, ul_ref, lh_ref, ll_ref)
    table = table_ref[...]
    twr, twi = twr_ref[...], twi_ref[...]
    mask = mask_ref[...]
    for row in range(ROWS):
        re_parts, im_parts = [], []
        for field in range(2):
            start = (2 * row + field) * SLOT
            re = spectra[start : start + SLOT, :LANES]
            im = spectra[start : start + SLOT, LANES:]
            re_parts.append(re * twr - im * twi)
            im_parts.append(re * twi + im * twr)
        twisted = jnp.concatenate(
            [jnp.concatenate(re_parts, axis=1), jnp.concatenate(im_parts, axis=1)], axis=0
        )
        high, low = split(twisted)
        hat = dot(table, jnp.concatenate([high, low, high], axis=0))
        mine = (x // 2) == row // HALF
        columns = jnp.concatenate(
            [
                jnp.where(
                    mine,
                    load_modes(w0_ref, field, row % HALF),
                    load_modes(w2_ref, field, row % HALF),
                )
                + hat[:, field * LANES : (field + 1) * LANES] * mask
                for field in range(2)
            ],
            axis=0,
        )
        out_ref[pl.ds(row, LANES, stride=ROWS), :] = columns.T


def to_rhs(x, grids, own, other, mask, tables):
    rows = 2 * ROWS * SLOT
    vmem = pl.BlockSpec(memory_space=pltpu.VMEM)
    return pl.pallas_call(
        modes_kernel,
        out_shape=jax.ShapeDtypeStruct((ROWS * LANES, LANES), jnp.float32),
        in_specs=[pl.BlockSpec(memory_space=pltpu.SMEM)] + [vmem] * 12,
        out_specs=vmem,
        scratch_shapes=[pltpu.VMEM((rows, 2 * LANES), jnp.bfloat16)] * 2,
        cost_estimate=pl.CostEstimate(
            flops=2 * rows * 256 * 256 * 3, bytes_accessed=2400000, transcendentals=0
        ),
        name="to_rhs",
    )(
        x,
        *grids,
        own,
        other,
        mask,
        tables["to_modes"],
        tables["twist_re"],
        tables["twist_im"],
        tables["lanes_h"],
        tables["lanes_l"],
    )


def matmul3(left, right, contract=((1,), (0,))):
    left_h, left_l = split(left)
    right_h, right_l = split(right)

    def one(u, v):
        return lax.dot_general(u, v, (contract, ((), ())), preferred_element_type=jnp.float32)

    return one(left_h, right_h) + one(left_h, right_l) + one(left_l, right_h)


def operator_kernel(inv_ref, mult_ref, high_ref, low_ref, g_ref, s_ref):
    nblocks, width, _ = inv_ref.shape
    eye = (
        lax.broadcasted_iota(jnp.int32, (width, width), 0)
        == lax.broadcasted_iota(jnp.int32, (width, width), 1)
    ).astype(jnp.float32)
    for j in range(nblocks):
        rows = pl.ds(j * width, width)
        if j:
            g_ref[rows, : j * width] = -matmul3(
                mult_ref[j - 1], g_ref[pl.ds((j - 1) * width, width), : j * width]
            )
        g_ref[rows, j * width : (j + 1) * width] = eye
    for j in reversed(range(nblocks)):
        rows = pl.ds(j * width, width)
        own = (j + 1) * width
        result = matmul3(inv_ref[j], g_ref[rows, :own])
        if j < nblocks - 1:
            result = jnp.concatenate(
                [result, jnp.zeros((width, (nblocks - 1 - j) * width), jnp.float32)], axis=1
            )
            result = result - matmul3(
                mult_ref[j], s_ref[pl.ds((j + 1) * width, width), :], ((0,), (0,))
            )
        s_ref[rows, :] = result
        high, low = split(result)
        high_ref[rows, :] = high
        low_ref[rows, :] = low


def solve_operator(block_inv, lower_mult):
    size = block_inv.shape[0] * block_inv.shape[1]
    return pl.pallas_call(
        operator_kernel,
        out_shape=[jax.ShapeDtypeStruct((size, size), jnp.bfloat16)] * 2,
        scratch_shapes=[pltpu.VMEM((size, size), jnp.float32)] * 2,
        cost_estimate=pl.CostEstimate(
            flops=2 * 55 * 3 * 128**3 * 4, bytes_accessed=3100000, transcendentals=0
        ),
        name="solve_operator",
    )(block_inv, lower_mult)


def solve_kernel(high_ref, low_ref, r_ref, out_ref, rh_ref):
    @pl.when(pl.program_id(0) == 0)
    def _():
        high, low = split(r_ref[...])
        rh_ref[:, :LANES] = high
        rh_ref[:, LANES:] = low

    both = dot(high_ref[...], rh_ref[...])
    out_ref[...] = both[:, :LANES] + both[:, LANES:] + dot(low_ref[...], rh_ref[:, :LANES])


def solve(operator, rhs):
    size = rhs.shape[0]
    steps = 3
    blocks = pl.BlockSpec((size // steps, size), lambda i: (i, 0))
    return pl.pallas_call(
        solve_kernel,
        out_shape=jax.ShapeDtypeStruct(rhs.shape, jnp.float32),
        grid=(steps,),
        in_specs=[blocks, blocks, pl.BlockSpec((size, LANES), lambda i: (0, 0))],
        out_specs=pl.BlockSpec((size // steps, LANES), lambda i: (i, 0)),
        scratch_shapes=[pltpu.VMEM((size, 2 * LANES), jnp.bfloat16)],
        name="solve",
    )(*operator, rhs)


def spread_kernel(s_ref, a_ref, b_ref):
    for row in range(ROWS):
        columns = s_ref[pl.ds(row, LANES, stride=ROWS), :].T
        for field, ref in enumerate((a_ref, b_ref)):
            base = field * 64
            ref[pl.ds(row * KEPT, KEPT), :] = columns[base : base + KEPT]
            ref[pl.ds(PARTS // 2 + row * KEPT, KEPT), :] = columns[base + 34 : base + 64]


def spread(solved):
    return pl.pallas_call(
        spread_kernel,
        out_shape=[jax.ShapeDtypeStruct((PARTS, LANES), jnp.float32)] * 2,
        name="spread",
    )(solved)


def exchange(rows, axes, count):
    sent = rows.reshape(count, 1, ROWS * LANES * LANES // count)
    return lax.all_to_all(sent, axes, 0, 0, tiled=True).reshape(rows.shape)


def swap(value, axis):
    return lax.ppermute(value, axis, [(0, 1), (1, 0)])


def body(field_a, field_b, keep_mask, block_inv, lower_mult):
    tables = {name: jnp.asarray(table) for name, table in build_tables().items()}
    y = lax.axis_index("y").astype(jnp.int32).reshape(1)
    x = 2 * y + lax.axis_index("c").astype(jnp.int32)
    send, own = prepare(y, field_a.reshape(PARTS, LANES), field_b.reshape(PARTS, LANES))
    two = swap(send, "y")
    one = swap(own, "c")
    grids = [to_grid(own, tables), to_grid(one, tables)]
    two, *grids = lax.optimization_barrier((two, *grids))
    three = swap(two, "c")
    grids += [to_grid(two, tables), to_grid(three, tables)]

    keep = keep_mask.astype(jnp.float32).reshape(KEPT, LANES)
    gap = jnp.zeros((2, LANES), jnp.float32)
    mask = jnp.concatenate([keep, gap, gap, keep], axis=0)
    rhs = to_rhs(x, grids, own, two, mask, tables)
    operator = solve_operator(block_inv, lower_mult)
    solved = solve(operator, exchange(rhs, ("wa", "y"), 256))
    new_a, new_b = spread(exchange(solved, "wa", 128))
    return (new_a.reshape(field_a.shape), new_b.reshape(field_b.shape))


def solution(mesh):
    wa, gx = mesh.devices.shape
    fine = Mesh(mesh.devices.reshape(wa, 2, gx // 2), ("wa", "y", "c"))
    fields = P(None, ("y", "c"), "wa", None)
    return jax.shard_map(
        body,
        mesh=fine,
        in_specs=(fields, fields, P(), P(), P()),
        out_specs=(fields, fields),
        check_vma=False,
    )
```

```python
import math

import jax
import jax.numpy as jnp
import ml_dtypes
import numpy as np
from jax import lax
from jax.experimental import pallas as pl
from jax.experimental.pallas import tpu as pltpu
from jax.sharding import Mesh
from jax.sharding import PartitionSpec as P

NL_COEFF = 0.25
BF16 = ml_dtypes.bfloat16

LANES = 128
OUTER = 45
KEPT = 30
ROWS = 6
HALF = ROWS // 2
SLOT = 48
PADDED = 64
JHALF = KEPT // 2
GROUPS = 16
PARTS = 2 * ROWS * KEPT


def split_np(table):
    high = table.astype(np.float32).astype(BF16)
    low = (table - high.astype(np.float64)).astype(np.float32).astype(BF16)
    return high, low


def place(jhalf, part):
    return 32 * jhalf + 16 * part + jhalf


def flip_bits(z):
    return int(f"{z:04b}"[::-1], 2)


def build_tables():
    modes = KEPT * LANES
    length = OUTER * LANES
    half = KEPT // 2
    kept = np.array([j if j < half else j + OUTER - KEPT for j in range(KEPT)])
    n1 = np.arange(OUTER)
    lane = np.arange(LANES)
    short = 2.0 * np.pi * ((n1[:, None] * kept[None, :]) % OUTER) / OUTER
    to_grid = np.zeros((2 * SLOT, 64))
    scale = 1.0 / math.sqrt(modes)
    re = np.array([place(j // half, 0) + j % half for j in range(KEPT)])
    im = np.array([place(j // half, 1) + j % half for j in range(KEPT)])
    to_grid[:OUTER, re] = np.cos(short) * scale
    to_grid[:OUTER, im] = -np.sin(short) * scale
    to_grid[SLOT : SLOT + OUTER, re] = np.sin(short) * scale
    to_grid[SLOT : SLOT + OUTER, im] = np.cos(short) * scale
    to_modes = np.zeros((64, 2 * SLOT))
    scale = NL_COEFF / math.sqrt(length)
    to_modes[re, :OUTER] = np.cos(short).T * scale
    to_modes[re, SLOT : SLOT + OUTER] = -np.sin(short).T * scale
    to_modes[im, :OUTER] = -np.sin(short).T * scale
    to_modes[im, SLOT : SLOT + OUTER] = -np.cos(short).T * scale
    twist = 2.0 * np.pi * (n1[:, None] * lane[None, :]) / length
    twist_re = np.zeros((SLOT, LANES), np.float32)
    twist_im = np.zeros((SLOT, LANES), np.float32)
    twist_re[:OUTER] = np.cos(twist)
    twist_im[:OUTER] = np.sin(twist)
    long = 2.0 * np.pi * ((lane[:, None] * lane[None, :]) % LANES) / LANES
    cos, sin = np.cos(long), np.sin(long)
    lanes = np.block([[cos, sin], [-sin, cos]])
    grid_h, grid_l = split_np(to_grid)
    modes_h, modes_l = split_np(to_modes)
    lanes_h, lanes_l = split_np(lanes)
    return dict(
        to_grid=np.concatenate([grid_h, grid_h, grid_l], axis=1),
        to_modes=np.concatenate([modes_h, modes_h, modes_l], axis=1),
        twist_re=twist_re,
        twist_im=twist_im,
        lanes_h=lanes_h,
        lanes_l=lanes_l,
    )


def call(kernel, out_shapes, args, name, scratch=(), scalars=0, flops=0, out_space=pltpu.VMEM):
    shapes = [jax.ShapeDtypeStruct(*shape) if out_space is None else out_space(*shape) for shape in out_shapes]
    args = [
        arg if i < scalars else pltpu.with_memory_space_constraint(arg, pltpu.VMEM)
        for i, arg in enumerate(args)
    ]
    smem = pl.BlockSpec(memory_space=pltpu.SMEM)
    vmem = pl.BlockSpec(memory_space=pltpu.VMEM)
    return pl.pallas_call(
        kernel,
        out_shape=shapes,
        in_specs=[smem] * scalars + [vmem] * (len(args) - scalars),
        out_specs=[vmem] * len(shapes),
        scratch_shapes=[pltpu.VMEM(*shape) for shape in scratch],
        compiler_params=pltpu.CompilerParams(vmem_limit_bytes=16 << 20),
        cost_estimate=pl.CostEstimate(flops=flops, bytes_accessed=1000000, transcendentals=0),
        name=name,
    )(*args)


def dot(left, right):
    return jnp.dot(left, right, preferred_element_type=jnp.float32)


def split(value):
    high = value.astype(jnp.bfloat16)
    low = (value - high.astype(jnp.float32)).astype(jnp.bfloat16)
    return high, low


def prepare_kernel(y_ref, a_ref, b_ref, send_ref, keep_ref):
    mine = y_ref[0]
    for half, out_ref in ((1 - mine, send_ref), (mine, keep_ref)):
        for field, ref in enumerate((a_ref, b_ref)):
            for i in range(HALF):
                row = (field * HALF + i) * PADDED
                for jhalf in range(2):
                    for part in range(2):
                        base = half * (HALF * KEPT) + part * (PARTS // 2) + i * KEPT
                        base = base + jhalf * (JHALF - 1)
                        out_ref[pl.ds(row + 32 * jhalf + 16 * part, 16), :] = ref[pl.ds(base, 16), :]


def prepare(y, field_a, field_b):
    shape = ((2 * HALF * PADDED, LANES), jnp.float32)
    return call(prepare_kernel, [shape, shape], (y, field_a, field_b), "prepare", scalars=1)


def load_modes(w_ref, field, i):
    return w_ref[pl.ds((field * HALF + i) * PADDED, PADDED), :]


def lane_transform(high_ref, low_ref, lanes_h_ref, lanes_l_ref):
    table = lanes_h_ref[...]
    return (
        dot(high_ref[...], table) + dot(low_ref[...], table) + dot(high_ref[...], lanes_l_ref[...])
    )


def grid_kernel(w_ref, table_ref, twr_ref, twi_ref, lh_ref, ll_ref, out_ref, uh_ref, ul_ref):
    table = table_ref[...]
    twr, twi = twr_ref[...], twi_ref[...]
    for row in range(HALF):
        modes = jnp.concatenate([load_modes(w_ref, 0, row), load_modes(w_ref, 1, row)], axis=1)
        high, low = split(modes)
        sums = dot(table, jnp.concatenate([high, low, high], axis=0))
        for field in range(2):
            lanes = slice(field * LANES, (field + 1) * LANES)
            re, im = sums[:SLOT, lanes], sums[SLOT:, lanes]
            twisted = jnp.concatenate([re * twr - im * twi, re * twi + im * twr], axis=1)
            high, low = split(twisted)
            rows = pl.ds((2 * row + field) * SLOT, SLOT)
            uh_ref[rows, :] = high
            ul_ref[rows, :] = low
    out_ref[...] = lane_transform(uh_ref, ul_ref, lh_ref, ll_ref)


def to_grid(own, tables):
    rows = 2 * HALF * SLOT
    names = ("to_grid", "twist_re", "twist_im", "lanes_h", "lanes_l")
    (grid,) = call(
        grid_kernel,
        [((rows, 2 * LANES), jnp.float32)],
        (own, *[tables[name] for name in names]),
        "to_grid",
        scratch=[((rows, 2 * LANES), jnp.bfloat16)] * 2,
        flops=2 * rows * 256 * 256 * 12,
    )
    return grid


def pairs_of(x, target):
    return [(j ^ x, ((target - j) % 4) ^ x) for j in range(4)]


def complex_product(left, right):
    return (left[0] * right[0] - left[1] * right[1], left[0] * right[1] + left[1] * right[0])


def modes_kernel(
    x_ref, g0, g1, g2, g3, w0_ref, w2_ref, keep_ref, table_ref, twr_ref, twi_ref, lh_ref, ll_ref,
    out_ref, uh_ref, ul_ref, mask_ref,
):
    grids = (g0, g1, g2, g3)
    x = x_ref[0]
    step_rows = 16

    def convolve(all_pairs):
        def step(index, carry):
            row = index // 3
            part = (index - row * 3) * step_rows
            base = row * 2 * SLOT + part

            def load(grid, field):
                rows = pl.ds(pl.multiple_of(base + field * SLOT, step_rows), step_rows)
                return (grid[rows, pl.ds(0, LANES)], grid[rows, pl.ds(LANES, LANES)])

            a = [load(grid, 0) for grid in grids]
            b = [load(grid, 1) for grid in grids]
            for target, pairs in enumerate(all_pairs):
                p = q = None
                for left, right in pairs:
                    ab = complex_product(a[left], b[right])
                    aa = complex_product(a[left], a[right])
                    bb = complex_product(b[left], b[right])
                    if p is None:
                        p = ab
                        q = (aa[0] - bb[0], aa[1] - bb[1])
                    else:
                        p = (p[0] + ab[0], p[1] + ab[1])
                        q = (q[0] + aa[0] - bb[0], q[1] + aa[1] - bb[1])
                for field, (re, im) in enumerate((p, q)):
                    high, low = split(jnp.concatenate([re, -im], axis=1))
                    start = base + (target * 2 * HALF + field) * SLOT
                    rows = pl.ds(pl.multiple_of(start, step_rows), step_rows)
                    uh_ref[rows, :] = high
                    ul_ref[rows, :] = low
            return carry

        lax.fori_loop(0, 3 * HALF, step, 0)

    for value in range(4):

        @pl.when(x == value)
        def _(value=value):
            convolve([pairs_of(value, 2 * target + value % 2) for target in range(2)])

    spectra = lane_transform(uh_ref, ul_ref, lh_ref, ll_ref)
    table = table_ref[...]
    twr, twi = twr_ref[...], twi_ref[...]
    mask_ref[...] = jnp.zeros_like(mask_ref)
    for jhalf in range(2):
        for part in range(2):
            flags = keep_ref[pl.ds(jhalf * JHALF, JHALF), :].astype(jnp.float32)
            mask_ref[pl.ds(place(jhalf, part), JHALF), :] = flags
    mask = mask_ref[...]

    def updated(target, i):
        re_parts, im_parts = [], []
        for field in range(2):
            start = ((target * HALF + i) * 2 + field) * SLOT
            re = spectra[start : start + SLOT, :LANES]
            im = spectra[start : start + SLOT, LANES:]
            re_parts.append(re * twr - im * twi)
            im_parts.append(re * twi + im * twr)
        twisted = jnp.concatenate(
            [jnp.concatenate(re_parts, axis=1), jnp.concatenate(im_parts, axis=1)], axis=0
        )
        high, low = split(twisted)
        hat = dot(table, jnp.concatenate([high, low, high], axis=0))
        mine = (x // 2) == target
        return [
            jnp.where(mine, load_modes(w0_ref, field, i), load_modes(w2_ref, field, i))
            + hat[:, field * LANES : (field + 1) * LANES] * mask
            for field in range(2)
        ]

    for i in range(HALF):
        blocks = updated(0, i) + updated(1, i)
        for jhalf in range(2):
            columns = jnp.concatenate(
                [block[32 * jhalf : 32 * jhalf + 32] for block in blocks], axis=0
            )
            out_ref[pl.ds(HALF * jhalf + i, LANES, stride=ROWS), :] = columns.T


def to_rhs(x, grids, own, other, keep, tables):
    rows = 2 * ROWS * SLOT
    names = ("to_modes", "twist_re", "twist_im", "lanes_h", "lanes_l")
    (rhs,) = call(
        modes_kernel,
        [((ROWS * LANES, LANES), jnp.float32)],
        (x, *grids, own, other, keep, *[tables[name] for name in names]),
        "to_rhs",
        scratch=[((rows, 2 * LANES), jnp.bfloat16)] * 2 + [((PADDED, LANES), jnp.float32)],
        scalars=1,
        flops=2 * rows * 256 * 256 * 12,
    )
    return rhs


def matmul3(left, right, contract=((1,), (0,))):
    left_h, left_l = split(left)
    right_h, right_l = split(right)

    def one(u, v):
        return lax.dot_general(u, v, (contract, ((), ())), preferred_element_type=jnp.float32)

    return one(left_h, right_h) + one(left_h, right_l) + one(left_l, right_h)


def operator_kernel(inv_ref, mult_ref, high_ref, low_ref, g_ref, s_ref):
    nblocks, width, _ = inv_ref.shape
    eye = (
        lax.broadcasted_iota(jnp.int32, (width, width), 0)
        == lax.broadcasted_iota(jnp.int32, (width, width), 1)
    ).astype(jnp.float32)
    for j in range(nblocks):
        rows = pl.ds(j * width, width)
        if j:
            g_ref[rows, : j * width] = -matmul3(
                mult_ref[j - 1], g_ref[pl.ds((j - 1) * width, width), : j * width]
            )
        g_ref[rows, j * width : (j + 1) * width] = eye
    for j in reversed(range(nblocks)):
        rows = pl.ds(j * width, width)
        own = (j + 1) * width
        result = matmul3(inv_ref[j], g_ref[rows, :own])
        if j < nblocks - 1:
            result = jnp.concatenate(
                [result, jnp.zeros((width, (nblocks - 1 - j) * width), jnp.float32)], axis=1
            )
            result = result - matmul3(
                mult_ref[j], s_ref[pl.ds((j + 1) * width, width), :], ((0,), (0,))
            )
        s_ref[rows, :] = result
        high, low = split(result)
        high_ref[rows, :] = high
        low_ref[rows, :] = low


def solve_operator(block_inv, lower_mult):
    size = block_inv.shape[0] * block_inv.shape[1]
    return call(
        operator_kernel,
        [((size, size), jnp.bfloat16)] * 2,
        (block_inv, lower_mult),
        "solve_operator",
        scratch=[((size, size), jnp.float32)] * 2,
        flops=2 * 55 * 3 * 128**3 * 4,
    )


def solve_kernel(high_ref, low_ref, r_ref, out_ref, rh_ref, n_ref):
    size = r_ref.shape[0]
    group = size // GROUPS
    for z in range(GROUPS):
        high, low = split(r_ref[pl.ds(flip_bits(z) * group, group), :])
        rh_ref[pl.ds(z * group, group), :LANES] = high
        rh_ref[pl.ds(z * group, group), LANES:] = low
    both = dot(high_ref[...], rh_ref[...])
    solved = both[:, :LANES] + both[:, LANES:] + dot(low_ref[...], rh_ref[:, :LANES])
    for z in range(GROUPS):
        n_ref[pl.ds(flip_bits(z) * group, group), :] = solved[z * group : (z + 1) * group]
    for i in range(HALF):
        first = n_ref[pl.ds(i, LANES, stride=ROWS), :]
        second = n_ref[pl.ds(HALF + i, LANES, stride=ROWS), :]
        for target in range(2):
            lanes = slice(target * 64, target * 64 + 64)
            out_ref[pl.ds(HALF * target + i, LANES, stride=ROWS), :] = jnp.concatenate(
                [first[:, lanes], second[:, lanes]], axis=1
            )


def solve(operator, rhs):
    size = rhs.shape[0]
    (solved,) = call(
        solve_kernel,
        [(rhs.shape, jnp.float32)],
        (*operator, rhs),
        "solve",
        scratch=[((size, 2 * LANES), jnp.bfloat16), (rhs.shape, jnp.float32)],
        flops=2 * size * size * 256 * 2,
    )
    return solved


def spread_kernel(s_ref, a_ref, b_ref):
    for jhalf in range(2):
        for i in range(HALF):
            columns = s_ref[pl.ds(HALF * jhalf + i, LANES, stride=ROWS), :].T
            for second in range(2):
                for field, ref in enumerate((a_ref, b_ref)):
                    for part in range(2):
                        start = second * 64 + field * 32 + part * 16 + jhalf
                        row = part * (PARTS // 2) + (i + HALF * second) * KEPT + jhalf * JHALF
                        ref[pl.ds(row, JHALF), :] = columns[start : start + JHALF]


def spread(solved):
    return call(
        spread_kernel, [((PARTS, LANES), jnp.float32)] * 2, (solved,), "spread", out_space=None
    )


ORDER = ("z0", "z1", "z2", "z3", "r", "y")


def exchange(rows):
    count = 2 * LANES
    sent = rows.reshape(count, 1, rows.size // count)
    return lax.all_to_all(sent, ORDER, 0, 0, tiled=True).reshape(rows.shape)


def swap(value, axis):
    return lax.ppermute(value, axis, [(0, 1), (1, 0)])


def body(field_a, field_b, keep_mask, block_inv, lower_mult):
    tables = {name: jnp.asarray(table) for name, table in build_tables().items()}
    y = lax.axis_index("y").astype(jnp.int32).reshape(1)
    x = 2 * y + lax.axis_index("c").astype(jnp.int32)
    send, own = prepare(y, field_a.reshape(PARTS, LANES), field_b.reshape(PARTS, LANES))
    two = swap(send, "y")
    one = swap(own, "c")
    grids = [to_grid(own, tables), to_grid(one, tables)]
    two, *grids = lax.optimization_barrier((two, *grids))
    three = swap(two, "c")
    grids += [to_grid(two, tables), to_grid(three, tables)]
    rhs = to_rhs(x, grids, own, two, keep_mask.reshape(KEPT, LANES), tables)
    operator = solve_operator(block_inv, lower_mult)
    new_a, new_b = spread(exchange(solve(operator, exchange(rhs))))
    return (new_a.reshape(field_a.shape), new_b.reshape(field_b.shape))


def solution(mesh):
    names = ("z3", "z2", "z1", "z0", "r", "y", "c")
    fine = Mesh(mesh.devices.reshape(2, 2, 2, 2, 8, 2, 2), names)
    fields = P(None, ("y", "c"), names[:5], None)
    return jax.shard_map(
        body,
        mesh=fine,
        in_specs=(fields, fields, P(), P(), P()),
        out_specs=(fields, fields),
        check_vma=False,
    )
```

```python
import math

import jax
import jax.numpy as jnp
import ml_dtypes
import numpy as np
from jax import lax
from jax.experimental import pallas as pl
from jax.experimental.pallas import tpu as pltpu
from jax.sharding import Mesh
from jax.sharding import PartitionSpec as P

NL_COEFF = 0.25
BF16 = ml_dtypes.bfloat16

LANES = 128
OUTER = 45
KEPT = 30
ROWS = 6
HALF = ROWS // 2
SLOT = 48
PADDED = 64
JHALF = KEPT // 2
PARTS = 2 * ROWS * KEPT


def split_np(table):
    high = table.astype(np.float32).astype(BF16)
    low = (table - high.astype(np.float64)).astype(np.float32).astype(BF16)
    return high, low


def place(jhalf, part):
    return 32 * jhalf + 16 * part + jhalf


def build_tables():
    modes = KEPT * LANES
    length = OUTER * LANES
    half = KEPT // 2
    kept = np.array([j if j < half else j + OUTER - KEPT for j in range(KEPT)])
    n1 = np.arange(OUTER)
    lane = np.arange(LANES)
    short = 2.0 * np.pi * ((n1[:, None] * kept[None, :]) % OUTER) / OUTER
    to_grid = np.zeros((2 * SLOT, 64))
    scale = 1.0 / math.sqrt(modes)
    re = np.array([place(j // half, 0) + j % half for j in range(KEPT)])
    im = np.array([place(j // half, 1) + j % half for j in range(KEPT)])
    to_grid[:OUTER, re] = np.cos(short) * scale
    to_grid[:OUTER, im] = -np.sin(short) * scale
    to_grid[SLOT : SLOT + OUTER, re] = np.sin(short) * scale
    to_grid[SLOT : SLOT + OUTER, im] = np.cos(short) * scale
    to_modes = np.zeros((64, 2 * SLOT))
    scale = NL_COEFF / math.sqrt(length)
    to_modes[re, :OUTER] = np.cos(short).T * scale
    to_modes[re, SLOT : SLOT + OUTER] = -np.sin(short).T * scale
    to_modes[im, :OUTER] = -np.sin(short).T * scale
    to_modes[im, SLOT : SLOT + OUTER] = -np.cos(short).T * scale
    twist = 2.0 * np.pi * (n1[:, None] * lane[None, :]) / length
    twist_re = np.zeros((SLOT, LANES), np.float32)
    twist_im = np.zeros((SLOT, LANES), np.float32)
    twist_re[:OUTER] = np.cos(twist)
    twist_im[:OUTER] = np.sin(twist)
    long = 2.0 * np.pi * ((lane[:, None] * lane[None, :]) % LANES) / LANES
    cos, sin = np.cos(long), np.sin(long)
    lanes = np.block([[cos, sin], [-sin, cos]])
    grid_h, grid_l = split_np(to_grid)
    modes_h, modes_l = split_np(to_modes)
    lanes_h, lanes_l = split_np(lanes)
    return dict(
        to_grid=np.concatenate([grid_h, grid_h, grid_l], axis=1),
        to_modes=np.concatenate([modes_h, modes_h, modes_l], axis=1),
        twist_re=twist_re,
        twist_im=twist_im,
        lanes_h=lanes_h,
        lanes_l=lanes_l,
    )


def call(kernel, out_shapes, args, name, scratch=(), scalars=0, flops=0, out_space=pltpu.VMEM):
    shapes = [jax.ShapeDtypeStruct(*shape) if out_space is None else out_space(*shape) for shape in out_shapes]
    args = [
        arg if i < scalars else pltpu.with_memory_space_constraint(arg, pltpu.VMEM)
        for i, arg in enumerate(args)
    ]
    smem = pl.BlockSpec(memory_space=pltpu.SMEM)
    vmem = pl.BlockSpec(memory_space=pltpu.VMEM)
    return pl.pallas_call(
        kernel,
        out_shape=shapes,
        in_specs=[smem] * scalars + [vmem] * (len(args) - scalars),
        out_specs=[vmem] * len(shapes),
        scratch_shapes=[pltpu.VMEM(*shape) for shape in scratch],
        compiler_params=pltpu.CompilerParams(vmem_limit_bytes=16 << 20),
        cost_estimate=pl.CostEstimate(flops=flops, bytes_accessed=1000000, transcendentals=0),
        name=name,
    )(*args)


def dot(left, right):
    return jnp.dot(left, right, preferred_element_type=jnp.float32)


def split(value):
    high = value.astype(jnp.bfloat16)
    low = (value - high.astype(jnp.float32)).astype(jnp.bfloat16)
    return high, low


def prepare_kernel(y_ref, a_ref, b_ref, send_ref, keep_ref):
    mine = y_ref[0]
    for half, out_ref in ((1 - mine, send_ref), (mine, keep_ref)):
        for field, ref in enumerate((a_ref, b_ref)):
            for i in range(HALF):
                row = (field * HALF + i) * PADDED
                for jhalf in range(2):
                    for part in range(2):
                        base = half * (HALF * KEPT) + part * (PARTS // 2) + i * KEPT
                        base = base + jhalf * (JHALF - 1)
                        out_ref[pl.ds(row + 32 * jhalf + 16 * part, 16), :] = ref[pl.ds(base, 16), :]


def prepare(y, field_a, field_b):
    shape = ((2 * HALF * PADDED, LANES), jnp.float32)
    return call(prepare_kernel, [shape, shape], (y, field_a, field_b), "prepare", scalars=1)


def load_modes(w_ref, field, i):
    return w_ref[pl.ds((field * HALF + i) * PADDED, PADDED), :]


def lane_transform(high_ref, low_ref, lanes_h_ref, lanes_l_ref):
    table = lanes_h_ref[...]
    return (
        dot(high_ref[...], table) + dot(low_ref[...], table) + dot(high_ref[...], lanes_l_ref[...])
    )


def grid_kernel(w_ref, table_ref, twr_ref, twi_ref, lh_ref, ll_ref, out_ref, uh_ref, ul_ref):
    table = table_ref[...]
    twr, twi = twr_ref[...], twi_ref[...]
    for row in range(HALF):
        modes = jnp.concatenate([load_modes(w_ref, 0, row), load_modes(w_ref, 1, row)], axis=1)
        high, low = split(modes)
        sums = dot(table, jnp.concatenate([high, low, high], axis=0))
        for field in range(2):
            lanes = slice(field * LANES, (field + 1) * LANES)
            re, im = sums[:SLOT, lanes], sums[SLOT:, lanes]
            twisted = jnp.concatenate([re * twr - im * twi, re * twi + im * twr], axis=1)
            high, low = split(twisted)
            rows = pl.ds((2 * row + field) * SLOT, SLOT)
            uh_ref[rows, :] = high
            ul_ref[rows, :] = low
    out_ref[...] = lane_transform(uh_ref, ul_ref, lh_ref, ll_ref)


def to_grid(own, tables):
    rows = 2 * HALF * SLOT
    names = ("to_grid", "twist_re", "twist_im", "lanes_h", "lanes_l")
    (grid,) = call(
        grid_kernel,
        [((rows, 2 * LANES), jnp.float32)],
        (own, *[tables[name] for name in names]),
        "to_grid",
        scratch=[((rows, 2 * LANES), jnp.bfloat16)] * 2,
        flops=2 * rows * 256 * 256 * 12,
    )
    return grid


def pairs_of(x, target):
    return [(j ^ x, ((target - j) % 4) ^ x) for j in range(4)]


def complex_product(left, right):
    return (left[0] * right[0] - left[1] * right[1], left[0] * right[1] + left[1] * right[0])


def modes_kernel(
    x_ref, g0, g1, g2, g3, w0_ref, w2_ref, keep_ref, table_ref, twr_ref, twi_ref, lh_ref, ll_ref,
    out_ref, uh_ref, ul_ref, mask_ref,
):
    grids = (g0, g1, g2, g3)
    x = x_ref[0]
    step_rows = 16

    def convolve(all_pairs):
        def step(index, carry):
            row = index // 3
            part = (index - row * 3) * step_rows
            base = row * 2 * SLOT + part

            def load(grid, field):
                rows = pl.ds(pl.multiple_of(base + field * SLOT, step_rows), step_rows)
                return (grid[rows, pl.ds(0, LANES)], grid[rows, pl.ds(LANES, LANES)])

            a = [load(grid, 0) for grid in grids]
            b = [load(grid, 1) for grid in grids]
            for target, pairs in enumerate(all_pairs):
                p = q = None
                for left, right in pairs:
                    ab = complex_product(a[left], b[right])
                    aa = complex_product(a[left], a[right])
                    bb = complex_product(b[left], b[right])
                    if p is None:
                        p = ab
                        q = (aa[0] - bb[0], aa[1] - bb[1])
                    else:
                        p = (p[0] + ab[0], p[1] + ab[1])
                        q = (q[0] + aa[0] - bb[0], q[1] + aa[1] - bb[1])
                for field, (re, im) in enumerate((p, q)):
                    high, low = split(jnp.concatenate([re, -im], axis=1))
                    start = base + (target * 2 * HALF + field) * SLOT
                    rows = pl.ds(pl.multiple_of(start, step_rows), step_rows)
                    uh_ref[rows, :] = high
                    ul_ref[rows, :] = low
            return carry

        lax.fori_loop(0, 3 * HALF, step, 0)

    for value in range(4):

        @pl.when(x == value)
        def _(value=value):
            convolve([pairs_of(value, 2 * target + value % 2) for target in range(2)])

    spectra = lane_transform(uh_ref, ul_ref, lh_ref, ll_ref)
    table = table_ref[...]
    twr, twi = twr_ref[...], twi_ref[...]
    mask_ref[...] = jnp.zeros_like(mask_ref)
    for jhalf in range(2):
        for part in range(2):
            flags = keep_ref[pl.ds(jhalf * JHALF, JHALF), :].astype(jnp.float32)
            mask_ref[pl.ds(place(jhalf, part), JHALF), :] = flags
    mask = mask_ref[...]

    def updated(target, i):
        re_parts, im_parts = [], []
        for field in range(2):
            start = ((target * HALF + i) * 2 + field) * SLOT
            re = spectra[start : start + SLOT, :LANES]
            im = spectra[start : start + SLOT, LANES:]
            re_parts.append(re * twr - im * twi)
            im_parts.append(re * twi + im * twr)
        twisted = jnp.concatenate(
            [jnp.concatenate(re_parts, axis=1), jnp.concatenate(im_parts, axis=1)], axis=0
        )
        high, low = split(twisted)
        hat = dot(table, jnp.concatenate([high, low, high], axis=0))
        mine = (x // 2) == target
        return [
            jnp.where(mine, load_modes(w0_ref, field, i), load_modes(w2_ref, field, i))
            + hat[:, field * LANES : (field + 1) * LANES] * mask
            for field in range(2)
        ]

    for i in range(HALF):
        blocks = updated(0, i) + updated(1, i)
        for jhalf in range(2):
            columns = jnp.concatenate(
                [block[32 * jhalf : 32 * jhalf + 32] for block in blocks], axis=0
            )
            out_ref[pl.ds(HALF * jhalf + i, LANES, stride=ROWS), :] = columns.T


def to_rhs(x, grids, own, other, keep, tables):
    rows = 2 * ROWS * SLOT
    names = ("to_modes", "twist_re", "twist_im", "lanes_h", "lanes_l")
    (rhs,) = call(
        modes_kernel,
        [((ROWS * LANES, LANES), jnp.float32)],
        (x, *grids, own, other, keep, *[tables[name] for name in names]),
        "to_rhs",
        scratch=[((rows, 2 * LANES), jnp.bfloat16)] * 2 + [((PADDED, LANES), jnp.float32)],
        scalars=1,
        flops=2 * rows * 256 * 256 * 12,
    )
    return rhs


def matmul3(left, right, contract=((1,), (0,))):
    left_h, left_l = split(left)
    right_h, right_l = split(right)

    def one(u, v):
        return lax.dot_general(u, v, (contract, ((), ())), preferred_element_type=jnp.float32)

    return one(left_h, right_h) + one(left_h, right_l) + one(left_l, right_h)


def operator_kernel(inv_ref, mult_ref, high_ref, low_ref, g_ref, s_ref):
    nblocks, width, _ = inv_ref.shape
    eye = (
        lax.broadcasted_iota(jnp.int32, (width, width), 0)
        == lax.broadcasted_iota(jnp.int32, (width, width), 1)
    ).astype(jnp.float32)
    for j in range(nblocks):
        rows = pl.ds(j * width, width)
        if j:
            g_ref[rows, : j * width] = -matmul3(
                mult_ref[j - 1], g_ref[pl.ds((j - 1) * width, width), : j * width]
            )
        g_ref[rows, j * width : (j + 1) * width] = eye
    for j in reversed(range(nblocks)):
        rows = pl.ds(j * width, width)
        own = (j + 1) * width
        result = matmul3(inv_ref[j], g_ref[rows, :own])
        if j < nblocks - 1:
            result = jnp.concatenate(
                [result, jnp.zeros((width, (nblocks - 1 - j) * width), jnp.float32)], axis=1
            )
            result = result - matmul3(
                mult_ref[j], s_ref[pl.ds((j + 1) * width, width), :], ((0,), (0,))
            )
        s_ref[rows, :] = result
        high, low = split(result)
        high_ref[rows, :] = high
        low_ref[rows, :] = low


def solve_operator(block_inv, lower_mult):
    size = block_inv.shape[0] * block_inv.shape[1]
    return call(
        operator_kernel,
        [((size, size), jnp.bfloat16)] * 2,
        (block_inv, lower_mult),
        "solve_operator",
        scratch=[((size, size), jnp.float32)] * 2,
        flops=2 * 55 * 3 * 128**3 * 4,
    )


def solve_kernel(high_ref, low_ref, r_ref, out_ref, n_ref):
    high, low = split(r_ref[...])
    both = dot(high_ref[...], jnp.concatenate([high, low], axis=1))
    n_ref[...] = both[:, :LANES] + both[:, LANES:] + dot(low_ref[...], high)
    for i in range(HALF):
        first = n_ref[pl.ds(i, LANES, stride=ROWS), :]
        second = n_ref[pl.ds(HALF + i, LANES, stride=ROWS), :]
        for target in range(2):
            lanes = slice(target * 64, target * 64 + 64)
            out_ref[pl.ds(HALF * target + i, LANES, stride=ROWS), :] = jnp.concatenate(
                [first[:, lanes], second[:, lanes]], axis=1
            )


def solve(operator, rhs):
    size = rhs.shape[0]
    (solved,) = call(
        solve_kernel,
        [(rhs.shape, jnp.float32)],
        (*operator, rhs),
        "solve",
        scratch=[(rhs.shape, jnp.float32)],
        flops=2 * size * size * 256 * 2,
    )
    return solved


def spread_kernel(s_ref, a_ref, b_ref):
    for jhalf in range(2):
        for i in range(HALF):
            columns = s_ref[pl.ds(HALF * jhalf + i, LANES, stride=ROWS), :].T
            for second in range(2):
                for field, ref in enumerate((a_ref, b_ref)):
                    for part in range(2):
                        start = second * 64 + field * 32 + part * 16 + jhalf
                        row = part * (PARTS // 2) + (i + HALF * second) * KEPT + jhalf * JHALF
                        ref[pl.ds(row, JHALF), :] = columns[start : start + JHALF]


def spread(solved):
    return call(
        spread_kernel, [((PARTS, LANES), jnp.float32)] * 2, (solved,), "spread", out_space=None
    )


ORDER = ("wa", "y")


def exchange(rows):
    count = 2 * LANES
    sent = rows.reshape(count, 1, rows.size // count)
    return lax.all_to_all(sent, ORDER, 0, 0, tiled=True).reshape(rows.shape)


def swap(value, axis):
    return lax.ppermute(value, axis, [(0, 1), (1, 0)])


def body(field_a, field_b, keep_mask, block_inv, lower_mult):
    tables = {name: jnp.asarray(table) for name, table in build_tables().items()}
    y = lax.axis_index("y").astype(jnp.int32).reshape(1)
    x = 2 * y + lax.axis_index("c").astype(jnp.int32)
    send, own = prepare(y, field_a.reshape(PARTS, LANES), field_b.reshape(PARTS, LANES))
    two = swap(send, "y")
    one = swap(own, "c")
    grids = [to_grid(own, tables), to_grid(one, tables)]
    two, *grids = lax.optimization_barrier((two, *grids))
    three = swap(two, "c")
    grids += [to_grid(two, tables), to_grid(three, tables)]
    rhs = to_rhs(x, grids, own, two, keep_mask.reshape(KEPT, LANES), tables)
    operator = solve_operator(block_inv, lower_mult)
    new_a, new_b = spread(exchange(solve(operator, exchange(rhs))))
    return (new_a.reshape(field_a.shape), new_b.reshape(field_b.shape))


def solution(mesh):
    wa, gx = mesh.devices.shape
    fine = Mesh(mesh.devices.reshape(wa, 2, gx // 2), ("wa", "y", "c"))
    fields = P(None, ("y", "c"), "wa", None)
    return jax.shard_map(
        body,
        mesh=fine,
        in_specs=(fields, fields, P(), P(), P()),
        out_specs=(fields, fields),
        check_vma=False,
    )
```

```python
import math

import jax
import jax.numpy as jnp
import ml_dtypes
import numpy as np
from jax import lax
from jax.experimental import pallas as pl
from jax.experimental.pallas import tpu as pltpu
from jax.sharding import Mesh
from jax.sharding import PartitionSpec as P

NL_COEFF = 0.25
BF16 = ml_dtypes.bfloat16

LANES = 128
OUTER = 45
KEPT = 30
ROWS = 6
HALF = ROWS // 2
SLOT = 48
PADDED = 64
HELD = PADDED // 2
GAP = HELD - KEPT
PARTS = 2 * ROWS * KEPT


def split_np(table):
    high = table.astype(np.float32).astype(BF16)
    low = (table - high.astype(np.float64)).astype(np.float32).astype(BF16)
    return high, low


def build_tables():
    modes = KEPT * LANES
    length = OUTER * LANES
    half = KEPT // 2
    kept = np.array([j if j < half else j + OUTER - KEPT for j in range(KEPT)])
    n1 = np.arange(OUTER)
    lane = np.arange(LANES)
    short = 2.0 * np.pi * ((n1[:, None] * kept[None, :]) % OUTER) / OUTER
    to_grid = np.zeros((2 * SLOT, 64))
    scale = 1.0 / math.sqrt(modes)
    re = np.arange(KEPT)
    im = HELD + GAP + re
    to_grid[:OUTER, re] = np.cos(short) * scale
    to_grid[:OUTER, im] = -np.sin(short) * scale
    to_grid[SLOT : SLOT + OUTER, re] = np.sin(short) * scale
    to_grid[SLOT : SLOT + OUTER, im] = np.cos(short) * scale
    to_modes = np.zeros((64, 2 * SLOT))
    scale = NL_COEFF / math.sqrt(length)
    to_modes[re, :OUTER] = np.cos(short).T * scale
    to_modes[re, SLOT : SLOT + OUTER] = -np.sin(short).T * scale
    to_modes[im, :OUTER] = -np.sin(short).T * scale
    to_modes[im, SLOT : SLOT + OUTER] = -np.cos(short).T * scale
    twist = 2.0 * np.pi * (n1[:, None] * lane[None, :]) / length
    twist_re = np.zeros((SLOT, LANES), np.float32)
    twist_im = np.zeros((SLOT, LANES), np.float32)
    twist_re[:OUTER] = np.cos(twist)
    twist_im[:OUTER] = np.sin(twist)
    long = 2.0 * np.pi * ((lane[:, None] * lane[None, :]) % LANES) / LANES
    cos, sin = np.cos(long), np.sin(long)
    lanes = np.block([[cos, sin], [-sin, cos]])
    grid_h, grid_l = split_np(to_grid)
    modes_h, modes_l = split_np(to_modes)
    lanes_h, lanes_l = split_np(lanes)
    return dict(
        to_grid=np.concatenate([grid_h, grid_h, grid_l], axis=1),
        to_modes=np.concatenate([modes_h, modes_h, modes_l], axis=1),
        twist_re=twist_re,
        twist_im=twist_im,
        lanes_h=lanes_h,
        lanes_l=lanes_l,
    )


def call(kernel, out_shapes, args, name, scratch=(), scalars=0, flops=0, inputs=pltpu.VMEM, on_chip=True):
    shapes = [pltpu.VMEM(*shape) if on_chip else jax.ShapeDtypeStruct(*shape) for shape in out_shapes]
    args = [
        arg if i < scalars else pltpu.with_memory_space_constraint(arg, inputs)
        for i, arg in enumerate(args)
    ]
    smem = pl.BlockSpec(memory_space=pltpu.SMEM)
    return pl.pallas_call(
        kernel,
        out_shape=shapes,
        in_specs=[smem] * scalars + [pl.BlockSpec(memory_space=inputs)] * (len(args) - scalars),
        out_specs=[pl.BlockSpec(memory_space=pltpu.VMEM)] * len(shapes),
        scratch_shapes=[pltpu.VMEM(*shape) if isinstance(shape, tuple) else shape for shape in scratch],
        compiler_params=pltpu.CompilerParams(vmem_limit_bytes=16 << 20),
        cost_estimate=pl.CostEstimate(flops=flops, bytes_accessed=1000000, transcendentals=0),
        name=name,
    )(*args)


def dot(left, right):
    return jnp.dot(left, right, preferred_element_type=jnp.float32)


def split(value):
    high = value.astype(jnp.bfloat16)
    low = (value - high.astype(jnp.float32)).astype(jnp.bfloat16)
    return high, low


def prepare_kernel(y_ref, a_hbm, b_hbm, *refs):
    count = (len(refs) - 5) // 2
    tables, (send_ref, keep_ref), copied = refs[:count], refs[count : count + 2], refs[count + 2 : -3]
    a_ref, b_ref, sems = refs[-3:]
    pairs = [(a_hbm, a_ref), (b_hbm, b_ref), *zip(tables, copied)]
    copies = [pltpu.make_async_copy(*pair, sems.at[i]) for i, pair in enumerate(pairs)]
    for copy in copies:
        copy.start()
    mine = y_ref[0]
    for copy in copies[:2]:
        copy.wait()
    for half, out_ref in ((1 - mine, send_ref), (mine, keep_ref)):
        for field, ref in enumerate((a_ref, b_ref)):
            for i in range(HALF):
                base = half * (HALF * KEPT) + i * KEPT
                row = (field * HALF + i) * PADDED
                out_ref[pl.ds(row, HELD), :] = ref[pl.ds(base, HELD), :]
                out_ref[pl.ds(row + HELD, HELD), :] = ref[pl.ds(base + PARTS // 2 - GAP, HELD), :]
    for copy in copies[2:]:
        copy.wait()


def prepare(y, field_a, field_b, tables):
    shape = ((2 * HALF * PADDED, LANES), jnp.float32)
    send, own, *copied = call(
        prepare_kernel,
        [shape, shape] + [(table.shape, table.dtype) for table in tables.values()],
        (y, field_a, field_b, *tables.values()),
        "prepare",
        scratch=[(field_a.shape, jnp.float32)] * 2 + [pltpu.SemaphoreType.DMA((2 + len(tables),))],
        scalars=1,
        inputs=pltpu.HBM,
    )
    return send, own, dict(zip(tables, copied))


def load_modes(w_ref, field, i):
    return w_ref[pl.ds((field * HALF + i) * PADDED, PADDED), :]


def lane_transform(high_ref, low_ref, lanes_h_ref, lanes_l_ref):
    table = lanes_h_ref[...]
    return (
        dot(high_ref[...], table) + dot(low_ref[...], table) + dot(high_ref[...], lanes_l_ref[...])
    )


def grid_kernel(w_ref, table_ref, twr_ref, twi_ref, lh_ref, ll_ref, out_ref, uh_ref, ul_ref):
    table = table_ref[...]
    twr, twi = twr_ref[...], twi_ref[...]
    for row in range(HALF):
        modes = jnp.concatenate([load_modes(w_ref, 0, row), load_modes(w_ref, 1, row)], axis=1)
        high, low = split(modes)
        sums = dot(table, jnp.concatenate([high, low, high], axis=0))
        for field in range(2):
            lanes = slice(field * LANES, (field + 1) * LANES)
            re, im = sums[:SLOT, lanes], sums[SLOT:, lanes]
            twisted = jnp.concatenate([re * twr - im * twi, re * twi + im * twr], axis=1)
            high, low = split(twisted)
            rows = pl.ds((2 * row + field) * SLOT, SLOT)
            uh_ref[rows, :] = high
            ul_ref[rows, :] = low
    out_ref[...] = lane_transform(uh_ref, ul_ref, lh_ref, ll_ref)


def to_grid(own, tables):
    rows = 2 * HALF * SLOT
    names = ("to_grid", "twist_re", "twist_im", "lanes_h", "lanes_l")
    (grid,) = call(
        grid_kernel,
        [((rows, 2 * LANES), jnp.float32)],
        (own, *[tables[name] for name in names]),
        "to_grid",
        scratch=[((rows, 2 * LANES), jnp.bfloat16)] * 2,
        flops=2 * rows * 256 * 256 * 12,
    )
    return grid


def pairs_of(x, target):
    return [(j ^ x, ((target - j) % 4) ^ x) for j in range(4)]


def complex_product(left, right):
    return (left[0] * right[0] - left[1] * right[1], left[0] * right[1] + left[1] * right[0])


def modes_kernel(
    x_ref, g0, g1, g2, g3, w0_ref, w2_ref, keep_ref, table_ref, twr_ref, twi_ref, lh_ref, ll_ref,
    out_ref, uh_ref, ul_ref, mask_ref,
):
    grids = (g0, g1, g2, g3)
    x = x_ref[0]
    step_rows = 16

    def convolve(all_pairs):
        def step(index, carry):
            row = index // 3
            part = (index - row * 3) * step_rows
            base = row * 2 * SLOT + part

            def load(grid, field):
                rows = pl.ds(pl.multiple_of(base + field * SLOT, step_rows), step_rows)
                return (grid[rows, pl.ds(0, LANES)], grid[rows, pl.ds(LANES, LANES)])

            a = [load(grid, 0) for grid in grids]
            b = [load(grid, 1) for grid in grids]
            for target, pairs in enumerate(all_pairs):
                p = q = None
                for left, right in pairs:
                    ab = complex_product(a[left], b[right])
                    aa = complex_product(a[left], a[right])
                    bb = complex_product(b[left], b[right])
                    if p is None:
                        p = ab
                        q = (aa[0] - bb[0], aa[1] - bb[1])
                    else:
                        p = (p[0] + ab[0], p[1] + ab[1])
                        q = (q[0] + aa[0] - bb[0], q[1] + aa[1] - bb[1])
                for field, (re, im) in enumerate((p, q)):
                    high, low = split(jnp.concatenate([re, -im], axis=1))
                    start = base + (target * 2 * HALF + field) * SLOT
                    rows = pl.ds(pl.multiple_of(start, step_rows), step_rows)
                    uh_ref[rows, :] = high
                    ul_ref[rows, :] = low
            return carry

        lax.fori_loop(0, 3 * HALF, step, 0)

    for value in range(4):

        @pl.when(x == value)
        def _(value=value):
            convolve([pairs_of(value, 2 * target + value % 2) for target in range(2)])

    spectra = lane_transform(uh_ref, ul_ref, lh_ref, ll_ref)
    table = table_ref[...]
    twr, twi = twr_ref[...], twi_ref[...]
    mask_ref[...] = jnp.zeros_like(mask_ref)
    flags = keep_ref[...].astype(jnp.float32)
    mask_ref[pl.ds(0, KEPT), :] = flags
    mask_ref[pl.ds(HELD + GAP, KEPT), :] = flags
    mask = mask_ref[...]

    def updated(target, i):
        re_parts, im_parts = [], []
        for field in range(2):
            start = ((target * HALF + i) * 2 + field) * SLOT
            re = spectra[start : start + SLOT, :LANES]
            im = spectra[start : start + SLOT, LANES:]
            re_parts.append(re * twr - im * twi)
            im_parts.append(re * twi + im * twr)
        twisted = jnp.concatenate(
            [jnp.concatenate(re_parts, axis=1), jnp.concatenate(im_parts, axis=1)], axis=0
        )
        high, low = split(twisted)
        hat = dot(table, jnp.concatenate([high, low, high], axis=0))
        mine = (x // 2) == target
        return [
            jnp.where(mine, load_modes(w0_ref, field, i), load_modes(w2_ref, field, i))
            + hat[:, field * LANES : (field + 1) * LANES] * mask
            for field in range(2)
        ]

    for row in range(ROWS):
        columns = jnp.concatenate(updated(row // HALF, row % HALF), axis=0)
        out_ref[pl.ds(row, LANES, stride=ROWS), :] = columns.T


def to_rhs(x, grids, own, other, tables):
    rows = 2 * ROWS * SLOT
    names = ("keep", "to_modes", "twist_re", "twist_im", "lanes_h", "lanes_l")
    (rhs,) = call(
        modes_kernel,
        [((ROWS * LANES, LANES), jnp.float32)],
        (x, *grids, own, other, *[tables[name] for name in names]),
        "to_rhs",
        scratch=[((rows, 2 * LANES), jnp.bfloat16)] * 2 + [((PADDED, LANES), jnp.float32)],
        scalars=1,
        flops=2 * rows * 256 * 256 * 12,
    )
    return rhs


def matmul3(left, right, contract=((1,), (0,))):
    left_h, left_l = split(left)
    right_h, right_l = split(right)

    def one(u, v):
        return lax.dot_general(u, v, (contract, ((), ())), preferred_element_type=jnp.float32)

    return one(left_h, right_h) + one(left_h, right_l) + one(left_l, right_h)


def operator_kernel(inv_ref, mult_ref, high_ref, low_ref, g_ref, s_ref):
    nblocks, width, _ = inv_ref.shape
    eye = (
        lax.broadcasted_iota(jnp.int32, (width, width), 0)
        == lax.broadcasted_iota(jnp.int32, (width, width), 1)
    ).astype(jnp.float32)
    for j in range(nblocks):
        rows = pl.ds(j * width, width)
        if j:
            g_ref[rows, : j * width] = -matmul3(
                mult_ref[j - 1], g_ref[pl.ds((j - 1) * width, width), : j * width]
            )
        g_ref[rows, j * width : (j + 1) * width] = eye
    for j in reversed(range(nblocks)):
        rows = pl.ds(j * width, width)
        own = (j + 1) * width
        result = matmul3(inv_ref[j], g_ref[rows, :own])
        if j < nblocks - 1:
            result = jnp.concatenate(
                [result, jnp.zeros((width, (nblocks - 1 - j) * width), jnp.float32)], axis=1
            )
            result = result - matmul3(
                mult_ref[j], s_ref[pl.ds((j + 1) * width, width), :], ((0,), (0,))
            )
        s_ref[rows, :] = result
        high, low = split(result)
        high_ref[rows, :] = high
        low_ref[rows, :] = low


def solve_operator(block_inv, lower_mult):
    size = block_inv.shape[0] * block_inv.shape[1]
    return call(
        operator_kernel,
        [((size, size), jnp.bfloat16)] * 2,
        (block_inv, lower_mult),
        "solve_operator",
        scratch=[((size, size), jnp.float32)] * 2,
        flops=2 * 55 * 3 * 128**3 * 4,
    )


def solve_kernel(high_ref, low_ref, r_ref, out_ref):
    high, low = split(r_ref[...])
    both = dot(high_ref[...], jnp.concatenate([high, low], axis=1))
    out_ref[...] = both[:, :LANES] + both[:, LANES:] + dot(low_ref[...], high)


def solve(operator, rhs):
    (solved,) = call(
        solve_kernel,
        [(rhs.shape, jnp.float32)],
        (*operator, rhs),
        "solve",
        flops=2 * rhs.shape[0] ** 2 * 256 * 2,
    )
    return solved


def spread_kernel(s_ref, a_ref, b_ref):
    for row in range(ROWS):
        columns = s_ref[pl.ds(row, LANES, stride=ROWS), :].T
        for field, ref in enumerate((a_ref, b_ref)):
            base = field * PADDED
            ref[pl.ds(row * KEPT, KEPT), :] = columns[base : base + KEPT]
            base = base + HELD + GAP
            ref[pl.ds(PARTS // 2 + row * KEPT, KEPT), :] = columns[base : base + KEPT]


def spread(solved):
    return call(
        spread_kernel, [((PARTS, LANES), jnp.float32)] * 2, (solved,), "spread", on_chip=False
    )


def exchange(rows, axes, count):
    sent = rows.reshape(count, 1, rows.size // count)
    return lax.all_to_all(sent, axes, 0, 0, tiled=True).reshape(rows.shape)


def swap(value, axis):
    return lax.ppermute(value, axis, [(0, 1), (1, 0)])


def body(field_a, field_b, keep_mask, block_inv, lower_mult):
    tables = {name: jnp.asarray(table) for name, table in build_tables().items()}
    tables["keep"] = keep_mask.reshape(KEPT, LANES)
    y = lax.axis_index("y").astype(jnp.int32).reshape(1)
    x = 2 * y + lax.axis_index("c").astype(jnp.int32)
    fields = (field_a.reshape(PARTS, LANES), field_b.reshape(PARTS, LANES))
    send, own, tables = prepare(y, *fields, tables)

    two = swap(send, "y")
    first = to_grid(own, tables)
    one = swap(own, "c")
    one, two, first = lax.optimization_barrier((one, two, first))
    three = swap(two, "c")
    grids = (first, *[to_grid(part, tables) for part in (one, two, three)])

    rhs = to_rhs(x, grids, own, two, tables)
    operator = solve_operator(block_inv, lower_mult)
    solved = solve(operator, exchange(rhs, ("wa", "y"), 2 * LANES))
    new_a, new_b = spread(exchange(solved, "wa", LANES))
    return (new_a.reshape(field_a.shape), new_b.reshape(field_b.shape))


def solution(mesh):
    wa, gx = mesh.devices.shape
    fine = Mesh(mesh.devices.reshape(wa, 2, gx // 2), ("wa", "y", "c"))
    fields = P(None, ("y", "c"), "wa", None)
    return jax.shard_map(
        body,
        mesh=fine,
        in_specs=(fields, fields, P(), P(), P()),
        out_specs=(fields, fields),
        check_vma=False,
    )
```

```python
import functools
import math

import jax
import jax.numpy as jnp
import ml_dtypes
import numpy as np
from jax import lax
from jax.experimental import pallas as pl
from jax.experimental.pallas import tpu as pltpu
from jax.sharding import Mesh
from jax.sharding import PartitionSpec as P

NL_COEFF = 0.25
BF16 = ml_dtypes.bfloat16

LANES = 128
OUTER = 45
KEPT = 30
ROWS = 6
HALF = ROWS // 2
SLOT = 48
PADDED = 64
HELD = PADDED // 2
GAP = HELD - KEPT
PARTS = 2 * ROWS * KEPT
BLOCKS = (2 * HALF * PADDED, LANES)


def split_np(table):
    high = table.astype(np.float32).astype(BF16)
    low = (table - high.astype(np.float64)).astype(np.float32).astype(BF16)
    return high, low


def build_tables():
    modes = KEPT * LANES
    length = OUTER * LANES
    half = KEPT // 2
    kept = np.array([j if j < half else j + OUTER - KEPT for j in range(KEPT)])
    n1 = np.arange(OUTER)
    lane = np.arange(LANES)
    short = 2.0 * np.pi * ((n1[:, None] * kept[None, :]) % OUTER) / OUTER
    to_grid = np.zeros((2 * SLOT, 64))
    scale = 1.0 / math.sqrt(modes)
    re = np.arange(KEPT)
    im = HELD + GAP + re
    to_grid[:OUTER, re] = np.cos(short) * scale
    to_grid[:OUTER, im] = -np.sin(short) * scale
    to_grid[SLOT : SLOT + OUTER, re] = np.sin(short) * scale
    to_grid[SLOT : SLOT + OUTER, im] = np.cos(short) * scale
    to_modes = np.zeros((64, 2 * SLOT))
    scale = NL_COEFF / math.sqrt(length)
    to_modes[re, :OUTER] = np.cos(short).T * scale
    to_modes[re, SLOT : SLOT + OUTER] = -np.sin(short).T * scale
    to_modes[im, :OUTER] = -np.sin(short).T * scale
    to_modes[im, SLOT : SLOT + OUTER] = -np.cos(short).T * scale
    twist = 2.0 * np.pi * (n1[:, None] * lane[None, :]) / length
    twist_re = np.zeros((SLOT, LANES), np.float32)
    twist_im = np.zeros((SLOT, LANES), np.float32)
    twist_re[:OUTER] = np.cos(twist)
    twist_im[:OUTER] = np.sin(twist)
    long = 2.0 * np.pi * ((lane[:, None] * lane[None, :]) % LANES) / LANES
    cos, sin = np.cos(long), np.sin(long)
    lanes = np.block([[cos, sin], [-sin, cos]])
    grid_h, grid_l = split_np(to_grid)
    modes_h, modes_l = split_np(to_modes)
    lanes_h, lanes_l = split_np(lanes)
    return dict(
        to_grid=np.concatenate([grid_h, grid_h, grid_l], axis=1),
        to_modes=np.concatenate([modes_h, modes_h, modes_l], axis=1),
        twist_re=twist_re,
        twist_im=twist_im,
        lanes_h=lanes_h,
        lanes_l=lanes_l,
    )


def call(kernel, out_shapes, args, name, scratch=(), scalars=0, flops=0, inputs=pltpu.VMEM, on_chip=True):
    shapes = [pltpu.VMEM(*shape) if on_chip else jax.ShapeDtypeStruct(*shape) for shape in out_shapes]
    spaces = inputs if isinstance(inputs, list) else [inputs] * (len(args) - scalars)
    args = [*args[:scalars], *map(pltpu.with_memory_space_constraint, args[scalars:], spaces)]
    specs = [pl.BlockSpec(memory_space=space) for space in [pltpu.SMEM] * scalars + spaces]
    return pl.pallas_call(
        kernel,
        out_shape=shapes,
        in_specs=specs,
        out_specs=[pl.BlockSpec(memory_space=pltpu.VMEM)] * len(shapes),
        scratch_shapes=[pltpu.VMEM(*shape) if isinstance(shape, tuple) else shape for shape in scratch],
        compiler_params=pltpu.CompilerParams(vmem_limit_bytes=16 << 20),
        cost_estimate=pl.CostEstimate(flops=flops, bytes_accessed=1000000, transcendentals=0),
        name=name,
    )(*args)


def dot(left, right):
    return jnp.dot(left, right, preferred_element_type=jnp.float32)


def split(value):
    high = value.astype(jnp.bfloat16)
    low = (value - high.astype(jnp.float32)).astype(jnp.bfloat16)
    return high, low


def pad_half(out_ref, refs, half):
    for field, ref in enumerate(refs):
        for i in range(HALF):
            base = half * (HALF * KEPT) + i * KEPT
            row = (field * HALF + i) * PADDED
            out_ref[pl.ds(row, HELD), :] = ref[pl.ds(base, HELD), :]
            out_ref[pl.ds(row + HELD, HELD), :] = ref[pl.ds(base + PARTS // 2 - GAP, HELD), :]


def send_kernel(y_ref, a_hbm, b_hbm, send_ref, a_ref, b_ref, sems):
    copies = [
        pltpu.make_async_copy(*pair, sems.at[i])
        for i, pair in enumerate([(a_hbm, a_ref), (b_hbm, b_ref)])
    ]
    for copy in copies:
        copy.start()
    for copy in copies:
        copy.wait()
    pad_half(send_ref, (a_ref, b_ref), 1 - y_ref[0])


def send_half(y, field_a, field_b):
    return call(
        send_kernel,
        [(BLOCKS, jnp.float32)] + [(field_a.shape, jnp.float32)] * 2,
        (y, field_a, field_b),
        "send_half",
        scratch=[pltpu.SemaphoreType.DMA((2,))],
        scalars=1,
        inputs=pltpu.HBM,
    )


def keep_kernel(y_ref, *refs):
    count = (len(refs) - 4) // 2
    a_ref, b_ref, tables = refs[count], refs[count + 1], refs[:count]
    keep_ref, copied, sems = refs[count + 2], refs[count + 3 : -1], refs[-1]
    copies = [
        pltpu.make_async_copy(*pair, sems.at[i]) for i, pair in enumerate(zip(tables, copied))
    ]
    for copy in copies:
        copy.start()
    pad_half(keep_ref, (a_ref, b_ref), y_ref[0])
    for copy in copies:
        copy.wait()


def keep_half(y, field_a, field_b, tables):
    own, *copied = call(
        keep_kernel,
        [(BLOCKS, jnp.float32)] + [(table.shape, table.dtype) for table in tables.values()],
        (y, *tables.values(), field_a, field_b),
        "keep_half",
        scratch=[pltpu.SemaphoreType.DMA((len(tables),))],
        scalars=1,
        inputs=[pltpu.HBM] * len(tables) + [pltpu.VMEM] * 2,
    )
    return own, dict(zip(tables, copied))


def load_modes(w_ref, field, i):
    return w_ref[pl.ds((field * HALF + i) * PADDED, PADDED), :]


def lane_transform(high_ref, low_ref, lanes_h_ref, lanes_l_ref):
    table = lanes_h_ref[...]
    return (
        dot(high_ref[...], table) + dot(low_ref[...], table) + dot(high_ref[...], lanes_l_ref[...])
    )


def grid_kernel(w_ref, table_ref, twr_ref, twi_ref, lh_ref, ll_ref, out_ref, uh_ref, ul_ref):
    table = table_ref[...]
    twr, twi = twr_ref[...], twi_ref[...]
    for row in range(HALF):
        modes = jnp.concatenate([load_modes(w_ref, 0, row), load_modes(w_ref, 1, row)], axis=1)
        high, low = split(modes)
        sums = dot(table, jnp.concatenate([high, low, high], axis=0))
        for field in range(2):
            lanes = slice(field * LANES, (field + 1) * LANES)
            re, im = sums[:SLOT, lanes], sums[SLOT:, lanes]
            twisted = jnp.concatenate([re * twr - im * twi, re * twi + im * twr], axis=1)
            high, low = split(twisted)
            rows = pl.ds((2 * row + field) * SLOT, SLOT)
            uh_ref[rows, :] = high
            ul_ref[rows, :] = low
    out_ref[...] = lane_transform(uh_ref, ul_ref, lh_ref, ll_ref)


def to_grid(own, tables):
    rows = 2 * HALF * SLOT
    names = ("to_grid", "twist_re", "twist_im", "lanes_h", "lanes_l")
    (grid,) = call(
        grid_kernel,
        [((rows, 2 * LANES), jnp.float32)],
        (own, *[tables[name] for name in names]),
        "to_grid",
        scratch=[((rows, 2 * LANES), jnp.bfloat16)] * 2,
        flops=2 * rows * 256 * 256 * 12,
    )
    return grid


def pairs_of(x, target):
    return [(j ^ x, ((target - j) % 4) ^ x) for j in range(4)]


def complex_product(left, right):
    return (left[0] * right[0] - left[1] * right[1], left[0] * right[1] + left[1] * right[0])


def plus(left, right):
    return (left[0] + right[0], left[1] + right[1])


def minus(left, right):
    return (left[0] - right[0], left[1] - right[1])


def add(terms):
    return functools.reduce(plus, terms)


def modes_kernel(
    x_ref, g0, g1, g2, g3, w0_ref, w2_ref, keep_ref, table_ref, twr_ref, twi_ref, lh_ref, ll_ref,
    out_ref, uh_ref, ul_ref, mask_ref,
):
    grids = (g0, g1, g2, g3)
    x = x_ref[0]
    step_rows = 16

    def convolve(all_pairs):
        def step(index, carry):
            row = index // 3
            part = (index - row * 3) * step_rows
            base = row * 2 * SLOT + part

            def load(grid, field):
                rows = pl.ds(pl.multiple_of(base + field * SLOT, step_rows), step_rows)
                return (grid[rows, pl.ds(0, LANES)], grid[rows, pl.ds(LANES, LANES)])

            a = [load(grid, 0) for grid in grids]
            b = [load(grid, 1) for grid in grids]
            for target, pairs in enumerate(all_pairs):
                p = add([complex_product(a[left], b[right]) for left, right in pairs])
                terms = []
                for left, right in pairs:
                    if left == right:
                        terms.append(complex_product(minus(a[left], b[left]), plus(a[left], b[left])))
                    elif left < right:
                        aa = complex_product(a[left], a[right])
                        both = minus(aa, complex_product(b[left], b[right]))
                        terms.append(plus(both, both))
                q = add(terms)
                for field, (re, im) in enumerate((p, q)):
                    high, low = split(jnp.concatenate([re, -im], axis=1))
                    start = base + (target * 2 * HALF + field) * SLOT
                    rows = pl.ds(pl.multiple_of(start, step_rows), step_rows)
                    uh_ref[rows, :] = high
                    ul_ref[rows, :] = low
            return carry

        lax.fori_loop(0, 3 * HALF, step, 0)

    for odd in range(2):

        @pl.when(x % 2 == odd)
        def _(odd=odd):
            convolve([pairs_of(odd, 2 * target + odd) for target in range(2)])

    spectra = lane_transform(uh_ref, ul_ref, lh_ref, ll_ref)
    table = table_ref[...]
    twr, twi = twr_ref[...], twi_ref[...]
    mask_ref[...] = jnp.zeros_like(mask_ref)
    flags = keep_ref[...].astype(jnp.float32)
    mask_ref[pl.ds(0, KEPT), :] = flags
    mask_ref[pl.ds(HELD + GAP, KEPT), :] = flags
    mask = mask_ref[...]

    def updated(target, i):
        re_parts, im_parts = [], []
        for field in range(2):
            start = ((target * HALF + i) * 2 + field) * SLOT
            re = spectra[start : start + SLOT, :LANES]
            im = spectra[start : start + SLOT, LANES:]
            re_parts.append(re * twr - im * twi)
            im_parts.append(re * twi + im * twr)
        twisted = jnp.concatenate(
            [jnp.concatenate(re_parts, axis=1), jnp.concatenate(im_parts, axis=1)], axis=0
        )
        high, low = split(twisted)
        hat = dot(table, jnp.concatenate([high, low, high], axis=0))
        mine = (x // 2) == target
        return [
            jnp.where(mine, load_modes(w0_ref, field, i), load_modes(w2_ref, field, i))
            + hat[:, field * LANES : (field + 1) * LANES] * mask
            for field in range(2)
        ]

    for row in range(ROWS):
        columns = jnp.concatenate(updated(row // HALF, row % HALF), axis=0)
        out_ref[pl.ds(row, LANES, stride=ROWS), :] = columns.T


def to_rhs(x, grids, own, other, tables):
    rows = 2 * ROWS * SLOT
    names = ("keep", "to_modes", "twist_re", "twist_im", "lanes_h", "lanes_l")
    (rhs,) = call(
        modes_kernel,
        [((ROWS * LANES, LANES), jnp.float32)],
        (x, *grids, own, other, *[tables[name] for name in names]),
        "to_rhs",
        scratch=[((rows, 2 * LANES), jnp.bfloat16)] * 2 + [((PADDED, LANES), jnp.float32)],
        scalars=1,
        flops=2 * rows * 256 * 256 * 12,
    )
    return rhs


def matmul3(left, right, contract=((1,), (0,))):
    left_h, left_l = split(left)
    right_h, right_l = split(right)

    def one(u, v):
        return lax.dot_general(u, v, (contract, ((), ())), preferred_element_type=jnp.float32)

    return one(left_h, right_h) + one(left_h, right_l) + one(left_l, right_h)


def operator_kernel(inv_ref, mult_ref, high_ref, low_ref, g_ref, s_ref):
    nblocks, width, _ = inv_ref.shape
    eye = (
        lax.broadcasted_iota(jnp.int32, (width, width), 0)
        == lax.broadcasted_iota(jnp.int32, (width, width), 1)
    ).astype(jnp.float32)
    for j in range(nblocks):
        rows = pl.ds(j * width, width)
        if j:
            g_ref[rows, : j * width] = -matmul3(
                mult_ref[j - 1], g_ref[pl.ds((j - 1) * width, width), : j * width]
            )
        g_ref[rows, j * width : (j + 1) * width] = eye
    for j in reversed(range(nblocks)):
        rows = pl.ds(j * width, width)
        own = (j + 1) * width
        result = matmul3(inv_ref[j], g_ref[rows, :own])
        if j < nblocks - 1:
            result = jnp.concatenate(
                [result, jnp.zeros((width, (nblocks - 1 - j) * width), jnp.float32)], axis=1
            )
            result = result - matmul3(
                mult_ref[j], s_ref[pl.ds((j + 1) * width, width), :], ((0,), (0,))
            )
        s_ref[rows, :] = result
        high, low = split(result)
        high_ref[rows, :] = high
        low_ref[rows, :] = low


def solve_operator(block_inv, lower_mult):
    size = block_inv.shape[0] * block_inv.shape[1]
    return call(
        operator_kernel,
        [((size, size), jnp.bfloat16)] * 2,
        (block_inv, lower_mult),
        "solve_operator",
        scratch=[((size, size), jnp.float32)] * 2,
        flops=2 * 55 * 3 * 128**3 * 4,
    )


def solve_kernel(high_ref, low_ref, r_ref, out_ref):
    high, low = split(r_ref[...])
    both = dot(high_ref[...], jnp.concatenate([high, low], axis=1))
    out_ref[...] = both[:, :LANES] + both[:, LANES:] + dot(low_ref[...], high)


def solve(operator, rhs):
    (solved,) = call(
        solve_kernel,
        [(rhs.shape, jnp.float32)],
        (*operator, rhs),
        "solve",
        flops=2 * rhs.shape[0] ** 2 * 256 * 2,
    )
    return solved


def spread_kernel(s_ref, a_ref, b_ref):
    for row in range(ROWS):
        columns = s_ref[pl.ds(row, LANES, stride=ROWS), :].T
        for field, ref in enumerate((a_ref, b_ref)):
            base = field * PADDED
            ref[pl.ds(row * KEPT, KEPT), :] = columns[base : base + KEPT]
            base = base + HELD + GAP
            ref[pl.ds(PARTS // 2 + row * KEPT, KEPT), :] = columns[base : base + KEPT]


def spread(solved):
    return call(
        spread_kernel, [((PARTS, LANES), jnp.float32)] * 2, (solved,), "spread", on_chip=False
    )


def exchange(rows, axes, count):
    sent = rows.reshape(count, 1, rows.size // count)
    return lax.all_to_all(sent, axes, 0, 0, tiled=True).reshape(rows.shape)


def swap(value, axis):
    return lax.ppermute(value, axis, [(0, 1), (1, 0)])


def body(field_a, field_b, keep_mask, block_inv, lower_mult):
    tables = {name: jnp.asarray(table) for name, table in build_tables().items()}
    tables["keep"] = keep_mask.reshape(KEPT, LANES)
    y = lax.axis_index("y").astype(jnp.int32).reshape(1)
    x = 2 * y + lax.axis_index("c").astype(jnp.int32)
    fields = (field_a.reshape(PARTS, LANES), field_b.reshape(PARTS, LANES))
    send, *fields = send_half(y, *fields)
    own, tables = keep_half(y, *fields, tables)

    two = swap(send, "y")
    first = to_grid(own, tables)
    one = swap(own, "c")
    one, two, first = lax.optimization_barrier((one, two, first))
    three = swap(two, "c")
    grids = (first, *[to_grid(part, tables) for part in (one, two, three)])

    rhs = to_rhs(x, grids, own, two, tables)
    operator = solve_operator(block_inv, lower_mult)
    solved = solve(operator, exchange(rhs, ("wa", "y"), 2 * LANES))
    new_a, new_b = spread(exchange(solved, "wa", LANES))
    return (new_a.reshape(field_a.shape), new_b.reshape(field_b.shape))


def solution(mesh):
    wa, gx = mesh.devices.shape
    fine = Mesh(mesh.devices.reshape(wa, 2, gx // 2), ("wa", "y", "c"))
    fields = P(None, ("y", "c"), "wa", None)
    return jax.shard_map(
        body,
        mesh=fine,
        in_specs=(fields, fields, P(), P(), P()),
        out_specs=(fields, fields),
        check_vma=False,
    )
```

```python
import functools
import math

import jax
import jax.numpy as jnp
import ml_dtypes
import numpy as np
from jax import lax
from jax.experimental import pallas as pl
from jax.experimental.pallas import tpu as pltpu
from jax.sharding import Mesh
from jax.sharding import PartitionSpec as P

NL_COEFF = 0.25
BF16 = ml_dtypes.bfloat16

LANES = 128
OUTER = 45
KEPT = 30
ROWS = 6
HALF = ROWS // 2
SLOT = 48
PADDED = 64
HELD = PADDED // 2
GAP = HELD - KEPT
PARTS = 2 * ROWS * KEPT
BLOCKS = (2 * HALF * PADDED, LANES)


def split_np(table):
    high = table.astype(np.float32).astype(BF16)
    low = (table - high.astype(np.float64)).astype(np.float32).astype(BF16)
    return high, low


def build_tables():
    modes = KEPT * LANES
    length = OUTER * LANES
    half = KEPT // 2
    kept = np.array([j if j < half else j + OUTER - KEPT for j in range(KEPT)])
    n1 = np.arange(OUTER)
    lane = np.arange(LANES)
    short = 2.0 * np.pi * ((n1[:, None] * kept[None, :]) % OUTER) / OUTER
    to_grid = np.zeros((2 * SLOT, 64))
    scale = 1.0 / math.sqrt(modes)
    re = np.arange(KEPT)
    im = HELD + GAP + re
    to_grid[:OUTER, re] = np.cos(short) * scale
    to_grid[:OUTER, im] = -np.sin(short) * scale
    to_grid[SLOT : SLOT + OUTER, re] = np.sin(short) * scale
    to_grid[SLOT : SLOT + OUTER, im] = np.cos(short) * scale
    to_modes = np.zeros((64, 2 * SLOT))
    scale = NL_COEFF / math.sqrt(length)
    to_modes[re, :OUTER] = np.cos(short).T * scale
    to_modes[re, SLOT : SLOT + OUTER] = -np.sin(short).T * scale
    to_modes[im, :OUTER] = -np.sin(short).T * scale
    to_modes[im, SLOT : SLOT + OUTER] = -np.cos(short).T * scale
    twist = 2.0 * np.pi * (n1[:, None] * lane[None, :]) / length
    twist_re = np.zeros((SLOT, LANES), np.float32)
    twist_im = np.zeros((SLOT, LANES), np.float32)
    twist_re[:OUTER] = np.cos(twist)
    twist_im[:OUTER] = np.sin(twist)
    long = 2.0 * np.pi * ((lane[:, None] * lane[None, :]) % LANES) / LANES
    cos, sin = np.cos(long), np.sin(long)
    lanes = np.block([[cos, sin], [-sin, cos]])
    grid_h, grid_l = split_np(to_grid)
    modes_h, modes_l = split_np(to_modes)
    lanes_h, lanes_l = split_np(lanes)
    return dict(
        to_grid=np.concatenate([grid_h, grid_h, grid_l], axis=1),
        to_modes=np.block([[modes_h, modes_h], [modes_l, np.zeros_like(modes_l)]]),
        twist_re=twist_re,
        twist_im=twist_im,
        lanes_h=lanes_h,
        lanes_l=lanes_l,
    )


def call(kernel, out_shapes, args, name, scratch=(), scalars=0, flops=0, inputs=pltpu.VMEM, on_chip=True):
    shapes = [pltpu.VMEM(*shape) if on_chip else jax.ShapeDtypeStruct(*shape) for shape in out_shapes]
    spaces = inputs if isinstance(inputs, list) else [inputs] * (len(args) - scalars)
    args = [*args[:scalars], *map(pltpu.with_memory_space_constraint, args[scalars:], spaces)]
    specs = [pl.BlockSpec(memory_space=space) for space in [pltpu.SMEM] * scalars + spaces]
    return pl.pallas_call(
        kernel,
        out_shape=shapes,
        in_specs=specs,
        out_specs=[pl.BlockSpec(memory_space=pltpu.VMEM)] * len(shapes),
        scratch_shapes=[pltpu.VMEM(*shape) if isinstance(shape, tuple) else shape for shape in scratch],
        compiler_params=pltpu.CompilerParams(vmem_limit_bytes=16 << 20),
        cost_estimate=pl.CostEstimate(flops=flops, bytes_accessed=1000000, transcendentals=0),
        name=name,
    )(*args)


def dot(left, right):
    return jnp.dot(left, right, preferred_element_type=jnp.float32)


def split(value):
    high = value.astype(jnp.bfloat16)
    low = (value - high.astype(jnp.float32)).astype(jnp.bfloat16)
    return high, low


def pad_half(out_ref, refs, half):
    for field, ref in enumerate(refs):
        for i in range(HALF):
            base = half * (HALF * KEPT) + i * KEPT
            row = (field * HALF + i) * PADDED
            out_ref[pl.ds(row, HELD), :] = ref[pl.ds(base, HELD), :]
            out_ref[pl.ds(row + HELD, HELD), :] = ref[pl.ds(base + PARTS // 2 - GAP, HELD), :]


def send_kernel(y_ref, a_hbm, b_hbm, send_ref, a_ref, b_ref, sems):
    copies = [
        pltpu.make_async_copy(*pair, sems.at[i])
        for i, pair in enumerate([(a_hbm, a_ref), (b_hbm, b_ref)])
    ]
    for copy in copies:
        copy.start()
    for copy in copies:
        copy.wait()
    pad_half(send_ref, (a_ref, b_ref), 1 - y_ref[0])


def send_half(y, field_a, field_b):
    return call(
        send_kernel,
        [(BLOCKS, jnp.float32)] + [(field_a.shape, jnp.float32)] * 2,
        (y, field_a, field_b),
        "send_half",
        scratch=[pltpu.SemaphoreType.DMA((2,))],
        scalars=1,
        inputs=pltpu.HBM,
    )


def keep_kernel(y_ref, *refs):
    count = (len(refs) - 4) // 2
    a_ref, b_ref, tables = refs[count], refs[count + 1], refs[:count]
    keep_ref, copied, sems = refs[count + 2], refs[count + 3 : -1], refs[-1]
    copies = [
        pltpu.make_async_copy(*pair, sems.at[i]) for i, pair in enumerate(zip(tables, copied))
    ]
    for copy in copies:
        copy.start()
    pad_half(keep_ref, (a_ref, b_ref), y_ref[0])
    for copy in copies:
        copy.wait()


def keep_half(y, field_a, field_b, tables):
    own, *copied = call(
        keep_kernel,
        [(BLOCKS, jnp.float32)] + [(table.shape, table.dtype) for table in tables.values()],
        (y, *tables.values(), field_a, field_b),
        "keep_half",
        scratch=[pltpu.SemaphoreType.DMA((len(tables),))],
        scalars=1,
        inputs=[pltpu.HBM] * len(tables) + [pltpu.VMEM] * 2,
    )
    return own, dict(zip(tables, copied))


def load_modes(w_ref, field, i):
    return w_ref[pl.ds((field * HALF + i) * PADDED, PADDED), :]


def lane_transform(high_ref, low_ref, lanes_h_ref, lanes_l_ref):
    table = lanes_h_ref[...]
    return (
        dot(high_ref[...], table) + dot(low_ref[...], table) + dot(high_ref[...], lanes_l_ref[...])
    )


def grid_kernel(w_ref, table_ref, twr_ref, twi_ref, lh_ref, ll_ref, out_ref, uh_ref, ul_ref):
    table = table_ref[...]
    twr, twi = twr_ref[...], twi_ref[...]
    for row in range(HALF):
        modes = jnp.concatenate([load_modes(w_ref, 0, row), load_modes(w_ref, 1, row)], axis=1)
        high, low = split(modes)
        sums = dot(table, jnp.concatenate([high, low, high], axis=0))
        for field in range(2):
            lanes = slice(field * LANES, (field + 1) * LANES)
            re, im = sums[:SLOT, lanes], sums[SLOT:, lanes]
            twisted = jnp.concatenate([re * twr - im * twi, re * twi + im * twr], axis=1)
            high, low = split(twisted)
            rows = pl.ds((2 * row + field) * SLOT, SLOT)
            uh_ref[rows, :] = high
            ul_ref[rows, :] = low
    out_ref[...] = lane_transform(uh_ref, ul_ref, lh_ref, ll_ref)


def to_grid(own, tables):
    rows = 2 * HALF * SLOT
    names = ("to_grid", "twist_re", "twist_im", "lanes_h", "lanes_l")
    (grid,) = call(
        grid_kernel,
        [((rows, 2 * LANES), jnp.float32)],
        (own, *[tables[name] for name in names]),
        "to_grid",
        scratch=[((rows, 2 * LANES), jnp.bfloat16)] * 2,
        flops=2 * rows * 256 * 256 * 12,
    )
    return grid


def pairs_of(x, target):
    return [(j ^ x, ((target - j) % 4) ^ x) for j in range(4)]


def complex_product(left, right):
    return (left[0] * right[0] - left[1] * right[1], left[0] * right[1] + left[1] * right[0])


def plus(left, right):
    return (left[0] + right[0], left[1] + right[1])


def minus(left, right):
    return (left[0] - right[0], left[1] - right[1])


def add(terms):
    return functools.reduce(plus, terms)


def modes_kernel(
    x_ref, g0, g1, g2, g3, w0_ref, w2_ref, keep_ref, table_ref, twr_ref, twi_ref, lh_ref, ll_ref,
    out_ref, uh_ref, ul_ref, mask_ref,
):
    grids = (g0, g1, g2, g3)
    x = x_ref[0]
    step_rows = 16

    def convolve(all_pairs):
        def step(index, carry):
            row = index // 3
            part = (index - row * 3) * step_rows
            base = row * 2 * SLOT + part

            def load(grid, field):
                rows = pl.ds(pl.multiple_of(base + field * SLOT, step_rows), step_rows)
                return (grid[rows, pl.ds(0, LANES)], grid[rows, pl.ds(LANES, LANES)])

            a = [load(grid, 0) for grid in grids]
            b = [load(grid, 1) for grid in grids]
            for target, pairs in enumerate(all_pairs):
                p = add([complex_product(a[left], b[right]) for left, right in pairs])
                terms = []
                for left, right in pairs:
                    if left == right:
                        terms.append(complex_product(minus(a[left], b[left]), plus(a[left], b[left])))
                    elif left < right:
                        aa = complex_product(a[left], a[right])
                        both = minus(aa, complex_product(b[left], b[right]))
                        terms.append(plus(both, both))
                q = add(terms)
                for field, (re, im) in enumerate((p, q)):
                    high, low = split(jnp.concatenate([re, -im], axis=1))
                    start = base + (target * 2 * HALF + field) * SLOT
                    rows = pl.ds(pl.multiple_of(start, step_rows), step_rows)
                    uh_ref[rows, :] = high
                    ul_ref[rows, :] = low
            return carry

        lax.fori_loop(0, 3 * HALF, step, 0)

    for odd in range(2):

        @pl.when(x % 2 == odd)
        def _(odd=odd):
            convolve([pairs_of(odd, 2 * target + odd) for target in range(2)])

    spectra = lane_transform(uh_ref, ul_ref, lh_ref, ll_ref)
    table = table_ref[...]
    twr, twi = twr_ref[...], twi_ref[...]
    mask_ref[...] = jnp.zeros_like(mask_ref)
    flags = keep_ref[...].astype(jnp.float32)
    mask_ref[pl.ds(0, KEPT), :] = flags
    mask_ref[pl.ds(HELD + GAP, KEPT), :] = flags
    mask = mask_ref[...]

    def updated(target, i):
        re_parts, im_parts = [], []
        for field in range(2):
            start = ((target * HALF + i) * 2 + field) * SLOT
            re = spectra[start : start + SLOT, :LANES]
            im = spectra[start : start + SLOT, LANES:]
            re_parts.append(re * twr - im * twi)
            im_parts.append(re * twi + im * twr)
        twisted = jnp.concatenate(
            [jnp.concatenate(re_parts, axis=1), jnp.concatenate(im_parts, axis=1)], axis=0
        )
        high, low = split(twisted)
        hat = dot(table, jnp.concatenate([high, low], axis=0))
        hat = hat[:PADDED] + hat[PADDED:]
        mine = (x // 2) == target
        return [
            jnp.where(mine, load_modes(w0_ref, field, i), load_modes(w2_ref, field, i))
            + hat[:, field * LANES : (field + 1) * LANES] * mask
            for field in range(2)
        ]

    for row in range(ROWS):
        columns = jnp.concatenate(updated(row // HALF, row % HALF), axis=0)
        out_ref[pl.ds(row, LANES, stride=ROWS), :] = columns.T


def to_rhs(x, grids, own, other, tables):
    rows = 2 * ROWS * SLOT
    names = ("keep", "to_modes", "twist_re", "twist_im", "lanes_h", "lanes_l")
    (rhs,) = call(
        modes_kernel,
        [((ROWS * LANES, LANES), jnp.float32)],
        (x, *grids, own, other, *[tables[name] for name in names]),
        "to_rhs",
        scratch=[((rows, 2 * LANES), jnp.bfloat16)] * 2 + [((PADDED, LANES), jnp.float32)],
        scalars=1,
        flops=2 * rows * 256 * 256 * 12,
    )
    return rhs


def matmul3(left, right, contract=((1,), (0,))):
    left_h, left_l = split(left)
    right_h, right_l = split(right)

    def one(u, v):
        return lax.dot_general(u, v, (contract, ((), ())), preferred_element_type=jnp.float32)

    return one(left_h, right_h) + one(left_h, right_l) + one(left_l, right_h)


def operator_kernel(inv_ref, mult_ref, high_ref, low_ref, g_ref, s_ref):
    nblocks, width, _ = inv_ref.shape
    eye = (
        lax.broadcasted_iota(jnp.int32, (width, width), 0)
        == lax.broadcasted_iota(jnp.int32, (width, width), 1)
    ).astype(jnp.float32)
    for j in range(nblocks):
        rows = pl.ds(j * width, width)
        if j:
            g_ref[rows, : j * width] = -matmul3(
                mult_ref[j - 1], g_ref[pl.ds((j - 1) * width, width), : j * width]
            )
        g_ref[rows, j * width : (j + 1) * width] = eye
    for j in reversed(range(nblocks)):
        rows = pl.ds(j * width, width)
        own = (j + 1) * width
        result = matmul3(inv_ref[j], g_ref[rows, :own])
        if j < nblocks - 1:
            result = jnp.concatenate(
                [result, jnp.zeros((width, (nblocks - 1 - j) * width), jnp.float32)], axis=1
            )
            result = result - matmul3(
                mult_ref[j], s_ref[pl.ds((j + 1) * width, width), :], ((0,), (0,))
            )
        s_ref[rows, :] = result
        high, low = split(result)
        high_ref[rows, :] = high
        low_ref[rows, :] = low


def solve_operator(block_inv, lower_mult):
    size = block_inv.shape[0] * block_inv.shape[1]
    return call(
        operator_kernel,
        [((size, size), jnp.bfloat16)] * 2,
        (block_inv, lower_mult),
        "solve_operator",
        scratch=[((size, size), jnp.float32)] * 2,
        flops=2 * 55 * 3 * 128**3 * 4,
    )


def solve_kernel(high_ref, low_ref, r_ref, out_ref):
    high, low = split(r_ref[...])
    both = dot(high_ref[...], jnp.concatenate([high, low], axis=1))
    out_ref[...] = both[:, :LANES] + both[:, LANES:] + dot(low_ref[...], high)


def solve(operator, rhs):
    (solved,) = call(
        solve_kernel,
        [(rhs.shape, jnp.float32)],
        (*operator, rhs),
        "solve",
        flops=2 * rhs.shape[0] ** 2 * 256 * 2,
    )
    return solved


def spread_kernel(s_ref, a_ref, b_ref):
    for row in range(ROWS):
        columns = s_ref[pl.ds(row, LANES, stride=ROWS), :].T
        for field, ref in enumerate((a_ref, b_ref)):
            base = field * PADDED
            ref[pl.ds(row * KEPT, KEPT), :] = columns[base : base + KEPT]
            base = base + HELD + GAP
            ref[pl.ds(PARTS // 2 + row * KEPT, KEPT), :] = columns[base : base + KEPT]


def spread(solved):
    return call(
        spread_kernel, [((PARTS, LANES), jnp.float32)] * 2, (solved,), "spread", on_chip=False
    )


def exchange(rows, axes, count):
    sent = rows.reshape(count, 1, rows.size // count)
    return lax.all_to_all(sent, axes, 0, 0, tiled=True).reshape(rows.shape)


def swap(value, axis):
    return lax.ppermute(value, axis, [(0, 1), (1, 0)])


def body(field_a, field_b, keep_mask, block_inv, lower_mult):
    tables = {name: jnp.asarray(table) for name, table in build_tables().items()}
    tables["keep"] = keep_mask.reshape(KEPT, LANES)
    y = lax.axis_index("y").astype(jnp.int32).reshape(1)
    x = 2 * y + lax.axis_index("c").astype(jnp.int32)
    fields = (field_a.reshape(PARTS, LANES), field_b.reshape(PARTS, LANES))
    send, *fields = send_half(y, *fields)
    own, tables = keep_half(y, *fields, tables)

    two = swap(send, "y")
    first = to_grid(own, tables)
    one = swap(own, "c")
    one, two, first = lax.optimization_barrier((one, two, first))
    three = swap(two, "c")
    grids = (first, *[to_grid(part, tables) for part in (one, two, three)])

    rhs = to_rhs(x, grids, own, two, tables)
    operator = solve_operator(block_inv, lower_mult)
    solved = solve(operator, exchange(rhs, ("wa", "y"), 2 * LANES))
    new_a, new_b = spread(exchange(solved, "wa", LANES))
    return (new_a.reshape(field_a.shape), new_b.reshape(field_b.shape))


def solution(mesh):
    wa, gx = mesh.devices.shape
    fine = Mesh(mesh.devices.reshape(wa, 2, gx // 2), ("wa", "y", "c"))
    fields = P(None, ("y", "c"), "wa", None)
    return jax.shard_map(
        body,
        mesh=fine,
        in_specs=(fields, fields, P(), P(), P()),
        out_specs=(fields, fields),
        check_vma=False,
    )
```

```python
import functools
import math

import jax
import jax.numpy as jnp
import ml_dtypes
import numpy as np
from jax import lax
from jax.experimental import pallas as pl
from jax.experimental.pallas import tpu as pltpu
from jax.sharding import Mesh
from jax.sharding import PartitionSpec as P

NL_COEFF = 0.25
BF16 = ml_dtypes.bfloat16

LANES = 128
OUTER = 45
KEPT = 30
ROWS = 6
HALF = ROWS // 2
SLOT = 48
PADDED = 64
HELD = PADDED // 2
GAP = HELD - KEPT
PARTS = 2 * ROWS * KEPT
BLOCKS = (2 * HALF * PADDED, LANES)


def split_np(table):
    high = table.astype(np.float32).astype(BF16)
    low = (table - high.astype(np.float64)).astype(np.float32).astype(BF16)
    return high, low


def build_tables():
    modes = KEPT * LANES
    length = OUTER * LANES
    half = KEPT // 2
    kept = np.array([j if j < half else j + OUTER - KEPT for j in range(KEPT)])
    n1 = np.arange(OUTER)
    lane = np.arange(LANES)
    short = 2.0 * np.pi * ((n1[:, None] * kept[None, :]) % OUTER) / OUTER
    to_grid = np.zeros((2 * SLOT, 64))
    scale = 1.0 / math.sqrt(modes)
    re = np.arange(KEPT)
    im = HELD + GAP + re
    to_grid[:OUTER, re] = np.cos(short) * scale
    to_grid[:OUTER, im] = -np.sin(short) * scale
    to_grid[SLOT : SLOT + OUTER, re] = np.sin(short) * scale
    to_grid[SLOT : SLOT + OUTER, im] = np.cos(short) * scale
    to_modes = np.zeros((64, 2 * SLOT))
    scale = NL_COEFF / math.sqrt(length)
    to_modes[re, :OUTER] = np.cos(short).T * scale
    to_modes[re, SLOT : SLOT + OUTER] = -np.sin(short).T * scale
    to_modes[im, :OUTER] = -np.sin(short).T * scale
    to_modes[im, SLOT : SLOT + OUTER] = -np.cos(short).T * scale
    twist = 2.0 * np.pi * (n1[:, None] * lane[None, :]) / length
    twist_re = np.zeros((SLOT, LANES), np.float32)
    twist_im = np.zeros((SLOT, LANES), np.float32)
    twist_re[:OUTER] = np.cos(twist)
    twist_im[:OUTER] = np.sin(twist)
    long = 2.0 * np.pi * ((lane[:, None] * lane[None, :]) % LANES) / LANES
    cos, sin = np.cos(long), np.sin(long)
    lanes = np.block([[cos, sin], [-sin, cos]])
    grid_h, grid_l = split_np(to_grid)
    modes_h, modes_l = split_np(to_modes)
    lanes_h, lanes_l = split_np(lanes)
    return dict(
        to_grid=np.concatenate([grid_h, grid_h, grid_l], axis=1),
        to_modes=np.block([[modes_h, modes_h], [modes_l, np.zeros_like(modes_l)]]),
        twist_re=twist_re,
        twist_im=twist_im,
        lanes_h=lanes_h,
        lanes_l=lanes_l,
    )


def call(kernel, out_shapes, args, name, scratch=(), scalars=0, flops=0, inputs=pltpu.VMEM, on_chip=True):
    shapes = [pltpu.VMEM(*shape) if on_chip else jax.ShapeDtypeStruct(*shape) for shape in out_shapes]
    spaces = inputs if isinstance(inputs, list) else [inputs] * (len(args) - scalars)
    args = [*args[:scalars], *map(pltpu.with_memory_space_constraint, args[scalars:], spaces)]
    specs = [pl.BlockSpec(memory_space=space) for space in [pltpu.SMEM] * scalars + spaces]
    return pl.pallas_call(
        kernel,
        out_shape=shapes,
        in_specs=specs,
        out_specs=[pl.BlockSpec(memory_space=pltpu.VMEM)] * len(shapes),
        scratch_shapes=[pltpu.VMEM(*shape) if isinstance(shape, tuple) else shape for shape in scratch],
        compiler_params=pltpu.CompilerParams(vmem_limit_bytes=16 << 20),
        cost_estimate=pl.CostEstimate(flops=flops, bytes_accessed=1000000, transcendentals=0),
        name=name,
    )(*args)


def dot(left, right):
    return jnp.dot(left, right, preferred_element_type=jnp.float32)


def split(value):
    high = value.astype(jnp.bfloat16)
    low = (value - high.astype(jnp.float32)).astype(jnp.bfloat16)
    return high, low


def pad_half(out_ref, refs, half):
    for field, ref in enumerate(refs):
        for i in range(HALF):
            base = half * (HALF * KEPT) + i * KEPT
            row = (field * HALF + i) * PADDED
            out_ref[pl.ds(row, HELD), :] = ref[pl.ds(base, HELD), :]
            out_ref[pl.ds(row + HELD, HELD), :] = ref[pl.ds(base + PARTS // 2 - GAP, HELD), :]


def send_kernel(y_ref, a_hbm, b_hbm, send_ref, a_ref, b_ref, sems):
    copies = [
        pltpu.make_async_copy(*pair, sems.at[i])
        for i, pair in enumerate([(a_hbm, a_ref), (b_hbm, b_ref)])
    ]
    for copy in copies:
        copy.start()
    for copy in copies:
        copy.wait()
    pad_half(send_ref, (a_ref, b_ref), 1 - y_ref[0])


def send_half(y, field_a, field_b):
    return call(
        send_kernel,
        [(BLOCKS, jnp.float32)] + [(field_a.shape, jnp.float32)] * 2,
        (y, field_a, field_b),
        "send_half",
        scratch=[pltpu.SemaphoreType.DMA((2,))],
        scalars=1,
        inputs=pltpu.HBM,
    )


def keep_kernel(y_ref, *refs):
    count = (len(refs) - 4) // 2
    a_ref, b_ref, tables = refs[count], refs[count + 1], refs[:count]
    keep_ref, copied, sems = refs[count + 2], refs[count + 3 : -1], refs[-1]
    copies = [
        pltpu.make_async_copy(*pair, sems.at[i]) for i, pair in enumerate(zip(tables, copied))
    ]
    for copy in copies:
        copy.start()
    pad_half(keep_ref, (a_ref, b_ref), y_ref[0])
    for copy in copies:
        copy.wait()


def keep_half(y, field_a, field_b, tables):
    own, *copied = call(
        keep_kernel,
        [(BLOCKS, jnp.float32)] + [(table.shape, table.dtype) for table in tables.values()],
        (y, *tables.values(), field_a, field_b),
        "keep_half",
        scratch=[pltpu.SemaphoreType.DMA((len(tables),))],
        scalars=1,
        inputs=[pltpu.HBM] * len(tables) + [pltpu.VMEM] * 2,
    )
    return own, dict(zip(tables, copied))


def load_modes(w_ref, field, i):
    return w_ref[pl.ds((field * HALF + i) * PADDED, PADDED), :]


def lane_transform(high_ref, low_ref, lanes_h_ref, lanes_l_ref):
    table = lanes_h_ref[...]
    return (
        dot(high_ref[...], table) + dot(low_ref[...], table) + dot(high_ref[...], lanes_l_ref[...])
    )


def grid_kernel(w_ref, table_ref, twr_ref, twi_ref, lh_ref, ll_ref, out_ref, uh_ref, ul_ref):
    table = table_ref[...]
    twr, twi = twr_ref[...], twi_ref[...]
    for row in range(HALF):
        modes = jnp.concatenate([load_modes(w_ref, 0, row), load_modes(w_ref, 1, row)], axis=1)
        high, low = split(modes)
        sums = dot(table, jnp.concatenate([high, low, high], axis=0))
        for field in range(2):
            lanes = slice(field * LANES, (field + 1) * LANES)
            re, im = sums[:SLOT, lanes], sums[SLOT:, lanes]
            twisted = jnp.concatenate([re * twr - im * twi, re * twi + im * twr], axis=1)
            high, low = split(twisted)
            rows = pl.ds((2 * row + field) * SLOT, SLOT)
            uh_ref[rows, :] = high
            ul_ref[rows, :] = low
    out_ref[...] = lane_transform(uh_ref, ul_ref, lh_ref, ll_ref)


def to_grid(own, tables):
    rows = 2 * HALF * SLOT
    names = ("to_grid", "twist_re", "twist_im", "lanes_h", "lanes_l")
    (grid,) = call(
        grid_kernel,
        [((rows, 2 * LANES), jnp.float32)],
        (own, *[tables[name] for name in names]),
        "to_grid",
        scratch=[((rows, 2 * LANES), jnp.bfloat16)] * 2,
        flops=2 * rows * 256 * 256 * 12,
    )
    return grid


def pairs_of(x, target):
    return [(j ^ x, ((target - j) % 4) ^ x) for j in range(4)]


def complex_product(left, right):
    return (left[0] * right[0] - left[1] * right[1], left[0] * right[1] + left[1] * right[0])


def plus(left, right):
    return (left[0] + right[0], left[1] + right[1])


def minus(left, right):
    return (left[0] - right[0], left[1] - right[1])


def add(terms):
    return functools.reduce(plus, terms)


def modes_kernel(
    x_ref, g0, g1, g2, g3, w0_ref, w2_ref, keep_ref, table_ref, twr_ref, twi_ref, lh_ref, ll_ref,
    out_ref, uh_ref, ul_ref, mask_ref,
):
    grids = (g0, g1, g2, g3)
    x = x_ref[0]
    step_rows = 16

    def convolve(all_pairs):
        def step(index, carry):
            row = index // 3
            part = (index - row * 3) * step_rows
            base = row * 2 * SLOT + part

            def load(grid, field):
                rows = pl.ds(pl.multiple_of(base + field * SLOT, step_rows), step_rows)
                return (grid[rows, pl.ds(0, LANES)], grid[rows, pl.ds(LANES, LANES)])

            a = [load(grid, 0) for grid in grids]
            b = [load(grid, 1) for grid in grids]
            for target, pairs in enumerate(all_pairs):
                p = add([complex_product(a[left], b[right]) for left, right in pairs])
                terms = []
                for left, right in pairs:
                    if left == right:
                        terms.append(complex_product(minus(a[left], b[left]), plus(a[left], b[left])))
                    elif left < right:
                        aa = complex_product(a[left], a[right])
                        both = minus(aa, complex_product(b[left], b[right]))
                        terms.append(plus(both, both))
                q = add(terms)
                for field, (re, im) in enumerate((p, q)):
                    high, low = split(jnp.concatenate([re, -im], axis=1))
                    start = base + (target * 2 * HALF + field) * SLOT
                    rows = pl.ds(pl.multiple_of(start, step_rows), step_rows)
                    uh_ref[rows, :] = high
                    ul_ref[rows, :] = low
            return carry

        lax.fori_loop(0, 3 * HALF, step, 0)

    for odd in range(2):

        @pl.when(x % 2 == odd)
        def _(odd=odd):
            convolve([pairs_of(odd, 2 * target + odd) for target in range(2)])

    spectra = lane_transform(uh_ref, ul_ref, lh_ref, ll_ref)
    table = table_ref[...]
    twr, twi = twr_ref[...], twi_ref[...]
    mask_ref[...] = jnp.zeros_like(mask_ref)
    flags = keep_ref[...].astype(jnp.float32)
    mask_ref[pl.ds(0, KEPT), :] = flags
    mask_ref[pl.ds(HELD + GAP, KEPT), :] = flags
    mask = mask_ref[...]

    def updated(target, i):
        re_parts, im_parts = [], []
        for field in range(2):
            start = ((target * HALF + i) * 2 + field) * SLOT
            re = spectra[start : start + SLOT, :LANES]
            im = spectra[start : start + SLOT, LANES:]
            re_parts.append(re * twr - im * twi)
            im_parts.append(re * twi + im * twr)
        twisted = jnp.concatenate(
            [jnp.concatenate(re_parts, axis=1), jnp.concatenate(im_parts, axis=1)], axis=0
        )
        high, low = split(twisted)
        hat = dot(table, jnp.concatenate([high, low], axis=0))
        hat = hat[:PADDED] + hat[PADDED:]
        mine = (x // 2) == target
        return [
            jnp.where(mine, load_modes(w0_ref, field, i), load_modes(w2_ref, field, i))
            + hat[:, field * LANES : (field + 1) * LANES] * mask
            for field in range(2)
        ]

    for row in range(ROWS):
        columns = jnp.concatenate(updated(row // HALF, row % HALF), axis=0)
        out_ref[pl.ds(row, LANES, stride=ROWS), :] = columns.T


def to_rhs(x, grids, own, other, tables):
    rows = 2 * ROWS * SLOT
    names = ("keep", "to_modes", "twist_re", "twist_im", "lanes_h", "lanes_l")
    (rhs,) = call(
        modes_kernel,
        [((ROWS * LANES, LANES), jnp.float32)],
        (x, *grids, own, other, *[tables[name] for name in names]),
        "to_rhs",
        scratch=[((rows, 2 * LANES), jnp.bfloat16)] * 2 + [((PADDED, LANES), jnp.float32)],
        scalars=1,
        flops=2 * rows * 256 * 256 * 12,
    )
    return rhs


def product_high(left, right, contract=((1,), (0,))):
    return lax.dot_general(
        left,
        right,
        (contract, ((), ())),
        precision=lax.Precision.HIGHEST,
        preferred_element_type=jnp.float32,
    )


def operator_kernel(inv_ref, mult_ref, high_ref, low_ref, g_ref, s_ref):
    nblocks, width, _ = inv_ref.shape
    eye = (
        lax.broadcasted_iota(jnp.int32, (width, width), 0)
        == lax.broadcasted_iota(jnp.int32, (width, width), 1)
    ).astype(jnp.float32)
    for j in range(nblocks):
        rows = pl.ds(j * width, width)
        if j:
            g_ref[rows, : j * width] = -product_high(
                mult_ref[j - 1], g_ref[pl.ds((j - 1) * width, width), : j * width]
            )
        g_ref[rows, j * width : (j + 1) * width] = eye
    for j in reversed(range(nblocks)):
        rows = pl.ds(j * width, width)
        own = (j + 1) * width
        result = product_high(inv_ref[j], g_ref[rows, :own])
        if j < nblocks - 1:
            result = jnp.concatenate(
                [result, jnp.zeros((width, (nblocks - 1 - j) * width), jnp.float32)], axis=1
            )
            result = result - product_high(
                mult_ref[j], s_ref[pl.ds((j + 1) * width, width), :], ((0,), (0,))
            )
        s_ref[rows, :] = result
        high, low = split(result)
        high_ref[rows, :] = high
        low_ref[rows, :] = low


def solve_operator(block_inv, lower_mult):
    size = block_inv.shape[0] * block_inv.shape[1]
    return call(
        operator_kernel,
        [((size, size), jnp.bfloat16)] * 2,
        (block_inv, lower_mult),
        "solve_operator",
        scratch=[((size, size), jnp.float32)] * 2,
        flops=2 * 55 * 3 * 128**3 * 4,
    )


def solve_kernel(high_ref, low_ref, r_ref, out_ref):
    high, low = split(r_ref[...])
    both = dot(high_ref[...], jnp.concatenate([high, low], axis=1))
    out_ref[...] = both[:, :LANES] + both[:, LANES:] + dot(low_ref[...], high)


def solve(operator, rhs):
    (solved,) = call(
        solve_kernel,
        [(rhs.shape, jnp.float32)],
        (*operator, rhs),
        "solve",
        flops=2 * rhs.shape[0] ** 2 * 256 * 2,
    )
    return solved


def spread_kernel(s_ref, a_ref, b_ref):
    for row in range(ROWS):
        columns = s_ref[pl.ds(row, LANES, stride=ROWS), :].T
        for field, ref in enumerate((a_ref, b_ref)):
            base = field * PADDED
            ref[pl.ds(row * KEPT, KEPT), :] = columns[base : base + KEPT]
            base = base + HELD + GAP
            ref[pl.ds(PARTS // 2 + row * KEPT, KEPT), :] = columns[base : base + KEPT]


def spread(solved):
    return call(
        spread_kernel, [((PARTS, LANES), jnp.float32)] * 2, (solved,), "spread", on_chip=False
    )


def exchange(rows, axes, count):
    sent = rows.reshape(count, 1, rows.size // count)
    return lax.all_to_all(sent, axes, 0, 0, tiled=True).reshape(rows.shape)


def swap(value, axis):
    return lax.ppermute(value, axis, [(0, 1), (1, 0)])


def body(field_a, field_b, keep_mask, block_inv, lower_mult):
    tables = {name: jnp.asarray(table) for name, table in build_tables().items()}
    tables["keep"] = keep_mask.reshape(KEPT, LANES)
    y = lax.axis_index("y").astype(jnp.int32).reshape(1)
    x = 2 * y + lax.axis_index("c").astype(jnp.int32)
    fields = (field_a.reshape(PARTS, LANES), field_b.reshape(PARTS, LANES))
    send, *fields = send_half(y, *fields)
    own, tables = keep_half(y, *fields, tables)

    two = swap(send, "y")
    first = to_grid(own, tables)
    one = swap(own, "c")
    one, two, first = lax.optimization_barrier((one, two, first))
    three = swap(two, "c")
    grids = (first, *[to_grid(part, tables) for part in (one, two, three)])

    rhs = to_rhs(x, grids, own, two, tables)
    operator = solve_operator(block_inv, lower_mult)
    solved = solve(operator, exchange(rhs, ("wa", "y"), 2 * LANES))
    new_a, new_b = spread(exchange(solved, "wa", LANES))
    return (new_a.reshape(field_a.shape), new_b.reshape(field_b.shape))


def solution(mesh):
    wa, gx = mesh.devices.shape
    fine = Mesh(mesh.devices.reshape(wa, 2, gx // 2), ("wa", "y", "c"))
    fields = P(None, ("y", "c"), "wa", None)
    return jax.shard_map(
        body,
        mesh=fine,
        in_specs=(fields, fields, P(), P(), P()),
        out_specs=(fields, fields),
        check_vma=False,
    )
```

```python
import functools
import math

import jax
import jax.numpy as jnp
import ml_dtypes
import numpy as np
from jax import lax
from jax.experimental import pallas as pl
from jax.experimental.pallas import tpu as pltpu
from jax.sharding import Mesh
from jax.sharding import PartitionSpec as P

NL_COEFF = 0.25
BF16 = ml_dtypes.bfloat16

LANES = 128
OUTER = 45
KEPT = 30
ROWS = 6
HALF = ROWS // 2
SLOT = 48
PADDED = 64
HELD = PADDED // 2
GAP = HELD - KEPT
PARTS = 2 * ROWS * KEPT
BLOCKS = (2 * HALF * PADDED, LANES)


def split_np(table):
    high = table.astype(np.float32).astype(BF16)
    low = (table - high.astype(np.float64)).astype(np.float32).astype(BF16)
    return high, low


def build_tables():
    modes = KEPT * LANES
    length = OUTER * LANES
    half = KEPT // 2
    kept = np.array([j if j < half else j + OUTER - KEPT for j in range(KEPT)])
    n1 = np.arange(OUTER)
    lane = np.arange(LANES)
    short = 2.0 * np.pi * ((n1[:, None] * kept[None, :]) % OUTER) / OUTER
    to_grid = np.zeros((2 * SLOT, 64))
    scale = 1.0 / math.sqrt(modes)
    re = np.arange(KEPT)
    im = HELD + GAP + re
    to_grid[:OUTER, re] = np.cos(short) * scale
    to_grid[:OUTER, im] = -np.sin(short) * scale
    to_grid[SLOT : SLOT + OUTER, re] = np.sin(short) * scale
    to_grid[SLOT : SLOT + OUTER, im] = np.cos(short) * scale
    to_modes = np.zeros((64, 2 * SLOT))
    scale = NL_COEFF / math.sqrt(length)
    to_modes[re, :OUTER] = np.cos(short).T * scale
    to_modes[re, SLOT : SLOT + OUTER] = -np.sin(short).T * scale
    to_modes[im, :OUTER] = -np.sin(short).T * scale
    to_modes[im, SLOT : SLOT + OUTER] = -np.cos(short).T * scale
    twist = 2.0 * np.pi * (n1[:, None] * lane[None, :]) / length
    twist_re = np.zeros((SLOT, LANES), np.float32)
    twist_im = np.zeros((SLOT, LANES), np.float32)
    twist_re[:OUTER] = np.cos(twist)
    twist_im[:OUTER] = np.sin(twist)
    long = 2.0 * np.pi * ((lane[:, None] * lane[None, :]) % LANES) / LANES
    cos, sin = np.cos(long), np.sin(long)
    lanes = np.block([[cos, sin], [-sin, cos]])
    grid_h, grid_l = split_np(to_grid)
    modes_h, modes_l = split_np(to_modes)
    lanes_h, lanes_l = split_np(lanes)
    return dict(
        to_grid=np.block([[grid_h, grid_h], [grid_l, np.zeros_like(grid_l)]]),
        to_modes=np.block([[modes_h, modes_h], [modes_l, np.zeros_like(modes_l)]]),
        twist_re=twist_re,
        twist_im=twist_im,
        lanes_h=lanes_h,
        lanes_l=lanes_l,
    )


def call(kernel, out_shapes, args, name, scratch=(), scalars=0, flops=0, inputs=pltpu.VMEM, on_chip=True):
    shapes = [pltpu.VMEM(*shape) if on_chip else jax.ShapeDtypeStruct(*shape) for shape in out_shapes]
    spaces = inputs if isinstance(inputs, list) else [inputs] * (len(args) - scalars)
    args = [*args[:scalars], *map(pltpu.with_memory_space_constraint, args[scalars:], spaces)]
    specs = [pl.BlockSpec(memory_space=space) for space in [pltpu.SMEM] * scalars + spaces]
    return pl.pallas_call(
        kernel,
        out_shape=shapes,
        in_specs=specs,
        out_specs=[pl.BlockSpec(memory_space=pltpu.VMEM)] * len(shapes),
        scratch_shapes=[pltpu.VMEM(*shape) if isinstance(shape, tuple) else shape for shape in scratch],
        compiler_params=pltpu.CompilerParams(vmem_limit_bytes=16 << 20),
        cost_estimate=pl.CostEstimate(flops=flops, bytes_accessed=1000000, transcendentals=0),
        name=name,
    )(*args)


def dot(left, right):
    return jnp.dot(left, right, preferred_element_type=jnp.float32)


def split(value):
    high = value.astype(jnp.bfloat16)
    low = (value - high.astype(jnp.float32)).astype(jnp.bfloat16)
    return high, low


def pad_half(out_ref, refs, half):
    for field, ref in enumerate(refs):
        for i in range(HALF):
            base = half * (HALF * KEPT) + i * KEPT
            row = (field * HALF + i) * PADDED
            out_ref[pl.ds(row, HELD), :] = ref[pl.ds(base, HELD), :]
            out_ref[pl.ds(row + HELD, HELD), :] = ref[pl.ds(base + PARTS // 2 - GAP, HELD), :]


def send_kernel(y_ref, a_hbm, b_hbm, send_ref, a_ref, b_ref, sems):
    copies = [
        pltpu.make_async_copy(*pair, sems.at[i])
        for i, pair in enumerate([(a_hbm, a_ref), (b_hbm, b_ref)])
    ]
    for copy in copies:
        copy.start()
    for copy in copies:
        copy.wait()
    pad_half(send_ref, (a_ref, b_ref), 1 - y_ref[0])


def send_half(y, field_a, field_b):
    return call(
        send_kernel,
        [(BLOCKS, jnp.float32)] + [(field_a.shape, jnp.float32)] * 2,
        (y, field_a, field_b),
        "send_half",
        scratch=[pltpu.SemaphoreType.DMA((2,))],
        scalars=1,
        inputs=pltpu.HBM,
    )


def keep_kernel(y_ref, *refs):
    count = (len(refs) - 4) // 2
    a_ref, b_ref, tables = refs[count], refs[count + 1], refs[:count]
    keep_ref, copied, sems = refs[count + 2], refs[count + 3 : -1], refs[-1]
    copies = [
        pltpu.make_async_copy(*pair, sems.at[i]) for i, pair in enumerate(zip(tables, copied))
    ]
    for copy in copies:
        copy.start()
    pad_half(keep_ref, (a_ref, b_ref), y_ref[0])
    for copy in copies:
        copy.wait()


def keep_half(y, field_a, field_b, tables):
    own, *copied = call(
        keep_kernel,
        [(BLOCKS, jnp.float32)] + [(table.shape, table.dtype) for table in tables.values()],
        (y, *tables.values(), field_a, field_b),
        "keep_half",
        scratch=[pltpu.SemaphoreType.DMA((len(tables),))],
        scalars=1,
        inputs=[pltpu.HBM] * len(tables) + [pltpu.VMEM] * 2,
    )
    return own, dict(zip(tables, copied))


def load_modes(w_ref, field, i):
    return w_ref[pl.ds((field * HALF + i) * PADDED, PADDED), :]


def lane_transform(high_ref, low_ref, lanes_h_ref, lanes_l_ref):
    table = lanes_h_ref[...]
    return (
        dot(high_ref[...], table) + dot(low_ref[...], table) + dot(high_ref[...], lanes_l_ref[...])
    )


def grid_kernel(w_ref, table_ref, twr_ref, twi_ref, lh_ref, ll_ref, out_ref, uh_ref, ul_ref):
    table = table_ref[...]
    twr, twi = twr_ref[...], twi_ref[...]
    for row in range(HALF):
        modes = jnp.concatenate([load_modes(w_ref, 0, row), load_modes(w_ref, 1, row)], axis=1)
        high, low = split(modes)
        sums = dot(table, jnp.concatenate([high, low], axis=0))
        sums = sums[: 2 * SLOT] + sums[2 * SLOT :]
        for field in range(2):
            lanes = slice(field * LANES, (field + 1) * LANES)
            re, im = sums[:SLOT, lanes], sums[SLOT:, lanes]
            twisted = jnp.concatenate([re * twr - im * twi, re * twi + im * twr], axis=1)
            high, low = split(twisted)
            rows = pl.ds((2 * row + field) * SLOT, SLOT)
            uh_ref[rows, :] = high
            ul_ref[rows, :] = low
    out_ref[...] = lane_transform(uh_ref, ul_ref, lh_ref, ll_ref)


def to_grid(own, tables):
    rows = 2 * HALF * SLOT
    names = ("to_grid", "twist_re", "twist_im", "lanes_h", "lanes_l")
    (grid,) = call(
        grid_kernel,
        [((rows, 2 * LANES), jnp.float32)],
        (own, *[tables[name] for name in names]),
        "to_grid",
        scratch=[((rows, 2 * LANES), jnp.bfloat16)] * 2,
        flops=2 * rows * 256 * 256 * 12,
    )
    return grid


def pairs_of(x, target):
    return [(j ^ x, ((target - j) % 4) ^ x) for j in range(4)]


def complex_product(left, right):
    return (left[0] * right[0] - left[1] * right[1], left[0] * right[1] + left[1] * right[0])


def plus(left, right):
    return (left[0] + right[0], left[1] + right[1])


def minus(left, right):
    return (left[0] - right[0], left[1] - right[1])


def add(terms):
    return functools.reduce(plus, terms)


def modes_kernel(
    x_ref, g0, g1, g2, g3, w0_ref, w2_ref, keep_ref, table_ref, twr_ref, twi_ref, lh_ref, ll_ref,
    out_ref, uh_ref, ul_ref, mask_ref,
):
    grids = (g0, g1, g2, g3)
    x = x_ref[0]
    step_rows = 16

    def convolve(all_pairs):
        def step(index, carry):
            row = index // 3
            part = (index - row * 3) * step_rows
            base = row * 2 * SLOT + part

            def load(grid, field):
                rows = pl.ds(pl.multiple_of(base + field * SLOT, step_rows), step_rows)
                return (grid[rows, pl.ds(0, LANES)], grid[rows, pl.ds(LANES, LANES)])

            a = [load(grid, 0) for grid in grids]
            b = [load(grid, 1) for grid in grids]
            for target, pairs in enumerate(all_pairs):
                p = add([complex_product(a[left], b[right]) for left, right in pairs])
                terms = []
                for left, right in pairs:
                    if left == right:
                        terms.append(complex_product(minus(a[left], b[left]), plus(a[left], b[left])))
                    elif left < right:
                        aa = complex_product(a[left], a[right])
                        both = minus(aa, complex_product(b[left], b[right]))
                        terms.append(plus(both, both))
                q = add(terms)
                for field, (re, im) in enumerate((p, q)):
                    high, low = split(jnp.concatenate([re, -im], axis=1))
                    start = base + (target * 2 * HALF + field) * SLOT
                    rows = pl.ds(pl.multiple_of(start, step_rows), step_rows)
                    uh_ref[rows, :] = high
                    ul_ref[rows, :] = low
            return carry

        lax.fori_loop(0, 3 * HALF, step, 0)

    for odd in range(2):

        @pl.when(x % 2 == odd)
        def _(odd=odd):
            convolve([pairs_of(odd, 2 * target + odd) for target in range(2)])

    spectra = lane_transform(uh_ref, ul_ref, lh_ref, ll_ref)
    table = table_ref[...]
    twr, twi = twr_ref[...], twi_ref[...]
    mask_ref[...] = jnp.zeros_like(mask_ref)
    flags = keep_ref[...].astype(jnp.float32)
    mask_ref[pl.ds(0, KEPT), :] = flags
    mask_ref[pl.ds(HELD + GAP, KEPT), :] = flags
    mask = mask_ref[...]

    def updated(target, i):
        re_parts, im_parts = [], []
        for field in range(2):
            start = ((target * HALF + i) * 2 + field) * SLOT
            re = spectra[start : start + SLOT, :LANES]
            im = spectra[start : start + SLOT, LANES:]
            re_parts.append(re * twr - im * twi)
            im_parts.append(re * twi + im * twr)
        twisted = jnp.concatenate(
            [jnp.concatenate(re_parts, axis=1), jnp.concatenate(im_parts, axis=1)], axis=0
        )
        high, low = split(twisted)
        hat = dot(table, jnp.concatenate([high, low], axis=0))
        hat = hat[:PADDED] + hat[PADDED:]
        mine = (x // 2) == target
        return [
            jnp.where(mine, load_modes(w0_ref, field, i), load_modes(w2_ref, field, i))
            + hat[:, field * LANES : (field + 1) * LANES] * mask
            for field in range(2)
        ]

    for row in range(ROWS):
        columns = jnp.concatenate(updated(row // HALF, row % HALF), axis=0)
        out_ref[pl.ds(row, LANES, stride=ROWS), :] = columns.T


def to_rhs(x, grids, own, other, tables):
    rows = 2 * ROWS * SLOT
    names = ("keep", "to_modes", "twist_re", "twist_im", "lanes_h", "lanes_l")
    (rhs,) = call(
        modes_kernel,
        [((ROWS * LANES, LANES), jnp.float32)],
        (x, *grids, own, other, *[tables[name] for name in names]),
        "to_rhs",
        scratch=[((rows, 2 * LANES), jnp.bfloat16)] * 2 + [((PADDED, LANES), jnp.float32)],
        scalars=1,
        flops=2 * rows * 256 * 256 * 12,
    )
    return rhs


def product_high(left, right, contract=((1,), (0,))):
    return lax.dot_general(
        left,
        right,
        (contract, ((), ())),
        precision=lax.Precision.HIGHEST,
        preferred_element_type=jnp.float32,
    )


def operator_kernel(inv_ref, mult_ref, high_ref, low_ref, g_ref, s_ref):
    nblocks, width, _ = inv_ref.shape
    eye = (
        lax.broadcasted_iota(jnp.int32, (width, width), 0)
        == lax.broadcasted_iota(jnp.int32, (width, width), 1)
    ).astype(jnp.float32)
    for j in range(nblocks):
        rows = pl.ds(j * width, width)
        if j:
            g_ref[rows, : j * width] = -product_high(
                mult_ref[j - 1], g_ref[pl.ds((j - 1) * width, width), : j * width]
            )
        g_ref[rows, j * width : (j + 1) * width] = eye
    for j in reversed(range(nblocks)):
        rows = pl.ds(j * width, width)
        own = (j + 1) * width
        result = product_high(inv_ref[j], g_ref[rows, :own])
        if j < nblocks - 1:
            result = jnp.concatenate(
                [result, jnp.zeros((width, (nblocks - 1 - j) * width), jnp.float32)], axis=1
            )
            result = result - product_high(
                mult_ref[j], s_ref[pl.ds((j + 1) * width, width), :], ((0,), (0,))
            )
        s_ref[rows, :] = result
        high, low = split(result)
        high_ref[rows, :] = high
        low_ref[rows, :] = low


def solve_operator(block_inv, lower_mult):
    size = block_inv.shape[0] * block_inv.shape[1]
    return call(
        operator_kernel,
        [((size, size), jnp.bfloat16)] * 2,
        (block_inv, lower_mult),
        "solve_operator",
        scratch=[((size, size), jnp.float32)] * 2,
        flops=2 * 55 * 3 * 128**3 * 4,
    )


def solve_kernel(high_ref, low_ref, r_ref, out_ref):
    high, low = split(r_ref[...])
    both = dot(high_ref[...], jnp.concatenate([high, low], axis=1))
    out_ref[...] = both[:, :LANES] + both[:, LANES:] + dot(low_ref[...], high)


def solve(operator, rhs):
    (solved,) = call(
        solve_kernel,
        [(rhs.shape, jnp.float32)],
        (*operator, rhs),
        "solve",
        flops=2 * rhs.shape[0] ** 2 * 256 * 2,
    )
    return solved


def spread_kernel(s_ref, a_ref, b_ref):
    for row in range(ROWS):
        columns = s_ref[pl.ds(row, LANES, stride=ROWS), :].T
        for field, ref in enumerate((a_ref, b_ref)):
            base = field * PADDED
            ref[pl.ds(row * KEPT, KEPT), :] = columns[base : base + KEPT]
            base = base + HELD + GAP
            ref[pl.ds(PARTS // 2 + row * KEPT, KEPT), :] = columns[base : base + KEPT]


def spread(solved):
    return call(
        spread_kernel, [((PARTS, LANES), jnp.float32)] * 2, (solved,), "spread", on_chip=False
    )


def exchange(rows, axes, count):
    sent = rows.reshape(count, 1, rows.size // count)
    return lax.all_to_all(sent, axes, 0, 0, tiled=True).reshape(rows.shape)


def swap(value, axis):
    return lax.ppermute(value, axis, [(0, 1), (1, 0)])


def body(field_a, field_b, keep_mask, block_inv, lower_mult):
    tables = {name: jnp.asarray(table) for name, table in build_tables().items()}
    tables["keep"] = keep_mask.reshape(KEPT, LANES)
    y = lax.axis_index("y").astype(jnp.int32).reshape(1)
    x = 2 * y + lax.axis_index("c").astype(jnp.int32)
    fields = (field_a.reshape(PARTS, LANES), field_b.reshape(PARTS, LANES))
    send, *fields = send_half(y, *fields)
    own, tables = keep_half(y, *fields, tables)

    two = swap(send, "y")
    first = to_grid(own, tables)
    one = swap(own, "c")
    one, two, first = lax.optimization_barrier((one, two, first))
    three = swap(two, "c")
    grids = (first, *[to_grid(part, tables) for part in (one, two, three)])

    rhs = to_rhs(x, grids, own, two, tables)
    operator = solve_operator(block_inv, lower_mult)
    solved = solve(operator, exchange(rhs, ("wa", "y"), 2 * LANES))
    new_a, new_b = spread(exchange(solved, "wa", LANES))
    return (new_a.reshape(field_a.shape), new_b.reshape(field_b.shape))


def solution(mesh):
    wa, gx = mesh.devices.shape
    fine = Mesh(mesh.devices.reshape(wa, 2, gx // 2), ("wa", "y", "c"))
    fields = P(None, ("y", "c"), "wa", None)
    return jax.shard_map(
        body,
        mesh=fine,
        in_specs=(fields, fields, P(), P(), P()),
        out_specs=(fields, fields),
        check_vma=False,
    )
```
